512 devices in a mesh: gy: 32 (over x, y, core), gx: 16 (over z).
Axes of the slice: x: 4, y: 4, z: 16, core: 2. Of those that a mesh axis runs over, the one named last changes fastest.
Arguments:
- pressure: float32 [8, 512, 2048], P(None, 'gy', 'gx'), may hold values from -6 to 6
- fluid_flux: float32 [8, 512, 2048], P(None, 'gy', 'gx'), may hold values from -5 to 5
- memory: float32 [4, 8, 512, 2048], P(None, None, 'gy', 'gx'), may hold values from -3 to 3
- lateral_faces: float32 [2, 8, 512, 2048], P(None, None, 'gy', 'gx'), may hold values from 100 to 1000
- vertical_faces: float32 [8, 512, 2048], P(None, 'gy', 'gx'), may hold values from 0.5 to 8
- relax_rates: float32 [4, 512, 2048], P(None, 'gy', 'gx'), may hold values from 0.1 to 4
Outputs:
- next_pressure: float32 [8, 512, 2048], P(None, 'gy', 'gx')
- next_flux: float32 [8, 512, 2048], P(None, 'gy', 'gx')
- next_memory: float32 [4, 8, 512, 2048], P(None, None, 'gy', 'gx')
The draws below stay inside these ranges and needn't reach their ends.
All inputs are finite; a program needn't handle non-finite values.
Results may differ from the reference program's by a relative error of at most 0.002.
Values sent between devices are 32-bit elements; how exact they have to be, the bound alone decides.
A program may use at most 192 MiB of HBM per device.

```python
import math
import jax
import jax.numpy as jnp
from jax import lax

NZ = 8
NX = 2048
NY = 512


def draw_fluid_flux(key, part):
    return jax.random.truncated_normal(key, -5.0, 5.0, (NZ, NY, NX), jnp.float32)


def level_of(stream_key, extent, cuts, low, top_value):
    def one(dim, blocks):
        heights = jax.random.uniform(jax.random.fold_in(jax.random.fold_in(stream_key, 6), dim), (blocks,), jnp.float32, low / len(cuts), top_value / len(cuts))
        return jnp.repeat(jnp.exp(heights), extent[dim] // blocks).reshape((-1,) + (1,) * (len(extent) - dim - 1))

    level = one(*cuts[0])
    for cut in cuts[1:]:
        level = level * one(*cut)
    return level


def gaussian(stream_key, dims, spread, bound, cuts=(), held_as=jnp.bfloat16):
    loudness = level_of(stream_key, dims, cuts, -0.22, 0.18) if cuts else 1.0
    array = jax.random.normal(stream_key, dims, jnp.float32) * spread * loudness
    return jnp.minimum(jnp.maximum(array, -bound), bound).astype(held_as)


def setup_inputs(seed: int = 0) -> dict:
    seeds = jax.random.split(jax.random.key(seed), 7)
    pressure = gaussian(seeds[0], (NZ, NY, NX), 1.0, 6.0, ((1, 32), (2, 16)), jnp.float32)
    fluid_flux = draw_fluid_flux(jax.random.fold_in(seeds[6], 71), 0)
    memory = gaussian(seeds[2], (4, NZ, NY, NX), 0.5, 3.0, ((2, 32), (3, 16)), jnp.float32)
    lateral_faces = jnp.clip(jnp.exp(math.log(1000.0) - 2.3025851 * jax.random.uniform(seeds[3], (2, NZ, NY, NX), jnp.float32) ** level_of(seeds[3], (2, NZ, NY, NX), ((2, 32), (3, 16)), -0.2, 0.2)), 100.0, 1000.0)
    vertical_faces = jnp.clip(jnp.exp(math.log(8.0) - 2.7725887 * jax.random.uniform(seeds[4], (NZ, NY, NX), jnp.float32) ** level_of(seeds[4], (NZ, NY, NX), ((1, 32), (2, 16)), -0.2, 0.2)), 0.5, 8.0)
    relax_rates = jnp.clip(jnp.exp(math.log(4.0) - 3.6888794 * jax.random.uniform(seeds[5], (4, NY, NX), jnp.float32) ** level_of(seeds[5], (4, NY, NX), ((1, 32), (2, 16)), -0.2, 0.2)), 0.1, 4.0)
    return dict(pressure=pressure, fluid_flux=fluid_flux, memory=memory, lateral_faces=lateral_faces, vertical_faces=vertical_faces, relax_rates=relax_rates)


def shift_low(values, line_axis):
    head_zero = jnp.zeros_like(lax.slice_in_dim(values, 0, 1, axis=line_axis))
    kept_cells = lax.slice_in_dim(values, 0, values.shape[line_axis] - 1, axis=line_axis)
    return jnp.concatenate([head_zero, kept_cells], axis=line_axis)

def shift_high(values, line_axis):
    tail_zero = jnp.zeros_like(lax.slice_in_dim(values, 0, 1, axis=line_axis))
    kept_cells = lax.slice_in_dim(values, 1, values.shape[line_axis], axis=line_axis)
    return jnp.concatenate([kept_cells, tail_zero], axis=line_axis)

def apply_line(field, faces, line_axis):
    face_low = shift_low(faces, line_axis)
    return faces * (shift_high(field, line_axis) - field) - face_low * (field - shift_low(field, line_axis))

def solve_lines(right_side, faces, line_axis):
    right_lines = jnp.moveaxis(right_side, line_axis, -1)
    face_high = jnp.moveaxis(faces, line_axis, -1)
    last_axis = face_high.ndim - 1
    face_low = shift_low(face_high, last_axis)
    lower_band = -0.5 * face_low
    main_band = 1.0 + 0.5 * (face_low + face_high)
    upper_band = jnp.concatenate([-0.5 * face_high[..., :-1], jnp.zeros_like(face_high[..., :1])], axis=last_axis)
    solved = lax.linalg.tridiagonal_solve(lower_band, main_band, upper_band, right_lines[..., None])[..., 0]
    return jnp.moveaxis(solved, -1, line_axis)

def relax_memory(memory, relax_rates, increment):
    target = increment / jnp.sqrt(1.0 + increment * increment)
    weight = relax_rates[:, None]
    return (memory + weight * target[None]) / (1.0 + weight)

def reference(pressure, fluid_flux, memory, lateral_faces, vertical_faces, relax_rates):
    explicit = apply_line(pressure, lateral_faces[0], 2) + apply_line(pressure, lateral_faces[1], 1)
    explicit = explicit + apply_line(pressure, vertical_faces, 0)
    source = fluid_flux - lax.optimization_barrier(jnp.sum(memory, axis=0))
    step_z = solve_lines(explicit + source, vertical_faces, 0)
    memory_z = relax_memory(memory, relax_rates, step_z)
    step_x = solve_lines(step_z, lateral_faces[0], 2)
    memory_x = relax_memory(memory_z, relax_rates, step_x)
    step_y = solve_lines(step_x, lateral_faces[1], 1)
    next_memory = relax_memory(memory_x, relax_rates, step_y)
    next_flux = fluid_flux - lax.optimization_barrier(jnp.sum(next_memory - memory, axis=0))
    return (pressure + step_y, next_flux, next_memory)
```

```python
from functools import partial

import jax
import jax.numpy as jnp
from jax import lax
from jax.experimental import pallas as pl
from jax.experimental.pallas import tpu as pltpu
from jax.sharding import PartitionSpec as P

MESH = pl.DeviceIdType.MESH


def rolled_low(a, s):
    return pltpu.roll(a, s, axis=1)


def rolled_high(a, s):
    return pltpu.roll(a, a.shape[1] - s, axis=1)


def major_low(a, s):
    return jnp.concatenate([a[a.shape[0] - s :], a[: a.shape[0] - s]], axis=0)


def major_high(a, s):
    return jnp.concatenate([a[s:], a[:s]], axis=0)


def factor(half, position, n, low, high, k1_ref, k2_ref, inv_ref, ends):
    first, last = position == 0, position == n - 1
    zero = jnp.zeros_like(half)
    link = jnp.where(last, zero, half)
    main = 1.0 + half + jnp.where(first, zero, low(half, 1))
    columns = []
    if ends:
        one = jnp.ones_like(half)
        columns = [jnp.where(first, one, zero), jnp.where(last, one, zero)]
    s, level = 1, 0
    while s < n:
        inverse = 1.0 / main
        k2 = link * high(inverse, s)
        scaled = link * inverse
        k1 = low(scaled, s)
        k1_ref[level] = k1
        k2_ref[level] = k2
        columns = [v + k1 * low(v, s) + k2 * high(v, s) for v in columns]
        main = main - low(link * scaled, s) - link * k2
        link = k2 * high(link, s)
        s, level = 2 * s, level + 1
    inverse = 1.0 / main
    inv_ref[...] = inverse
    return [v * inverse for v in columns]


def reduce_lines(right, n, low, high, k1_ref, k2_ref, inv_ref):
    s, level = 1, 0
    while s < n:
        right = right + k1_ref[level] * low(right, s) + k2_ref[level] * high(right, s)
        s, level = 2 * s, level + 1
    return right * inv_ref[...]


def join(one, two):
    g1, c1, w1, h1 = one
    g2, c2, w2, h2 = two
    e1 = 1.0 - w1 * h1
    gh = g2 * h1
    d = 1.0 / (1.0 + gh * e1)
    up, down = c1 * h1 * d, c2 * h1 * d
    block = (g1 + up * gh * c1, up * c2, w2 - down * e1 * c2, h2)
    return block, (gh, up, e1, down)


def join_values(factors, one, two):
    gh, up, e1, down = factors
    f1, l1 = one
    f2, l2 = two
    return f1 + up * (f2 + gh * l1), l2 + down * (l1 - e1 * f2)


def join_all(blocks, combine):
    while len(blocks) > 1:
        blocks = [combine(blocks[k], blocks[k + 1]) for k in range(0, len(blocks), 2)]
    return blocks[0]


def below(blocks, own):
    w, h = jnp.zeros_like(own[0]), jnp.zeros_like(own[0])
    factors = []
    for counts, (gj, cj, wj, hj) in blocks:
        a = h * (1.0 - w * h)
        t = cj / (1.0 + gj * a)
        kappa, eps = t * h, t * a
        factors.append((kappa, eps))
        w = jnp.where(counts, wj - cj * eps, w)
        h = jnp.where(counts, hj, h)
    return (w, h), factors


def above(blocks, own):
    g = jnp.zeros_like(own[0])
    factors = []
    for counts, (gj, cj, wj, hj) in blocks:
        ch, gh = cj * hj, g * hj
        kappa = ch / (1.0 + gh * (1.0 - wj * hj))
        factors.append((kappa, kappa * gh))
        g = jnp.where(counts, gj + ch * kappa * g, g)
    return g, factors


def own_factors(own, low_state, g_above):
    g, c, w, h = own
    w_low, h_low = low_state
    a = h_low * (1.0 - w_low * h_low)
    gh = g_above * h
    p = h / (1.0 + gh)
    q = gh * p
    r1, r2, ca, cq = 1.0 + g * a, 1.0 - w * q, c * a, c * q
    inverse = 1.0 / (r1 * r2 + ca * cq)
    return (h_low, a, p, q, r1 * inverse, r2 * inverse, ca * inverse, cq * inverse)


def inflow(own, factors, mine, e_low, f_high):
    g, c, w, _ = own
    h_low, a, p, q, r1, r2, ca, cq = factors
    u, v = h_low * e_low, p * f_high
    s1 = mine[0] + g * u + c * v
    s2 = mine[1] + c * u + w * v
    return u - a * (r2 * s1 + cq * s2), v + q * (r1 * s2 - ca * s1)


class Ring:
    def __init__(self, buffer, sems, size, index, device):
        self.buffer, self.size, self.index, self.device = buffer, size, index, device
        self.send, self.receive = sems

    def copy(self, k):
        slot = self.buffer.at[self.index]
        return pltpu.make_async_remote_copy(
            src_ref=slot,
            dst_ref=slot,
            send_sem=self.send.at[k - 1],
            recv_sem=self.receive.at[k - 1],
            device_id=self.device(lax.rem(self.index + k, self.size)),
            device_id_type=MESH,
        )

    def each(self, act):
        def turn(k, carry):
            act(self.copy(k))
            return carry

        lax.fori_loop(1, self.size, turn, 0)

    def start(self):
        self.each(lambda copy: copy.start())

    def arrive(self):
        self.each(lambda copy: copy.wait_recv())

    def finish(self):
        self.each(lambda copy: copy.wait_send())


def kernel(
    sizes,
    pressure_in, flux_in, memory_in, lateral_in, vertical_in, relax_in,
    pressure_out, flux_out, memory_out,
    p_ref, f_ref, m_ref, kx_ref, ky_ref, kz_ref, relax_ref,
    np_ref, nf_ref, nm_ref,
    x1_ref, x2_ref, xi_ref, vt_ref, wt_ref,
    y1_ref, y2_ref, yi_ref, vs_ref, ws_ref,
    z1_ref, z2_ref, zi_ref,
    e_ref, iw_ref, wi_ref,
    east_out, west_out, east_in, west_in,
    north_out, south_out, north_in, south_in,
    xc_ref, xv_ref, yc_ref, yv_ref, yc2_ref, yv2_ref,
    xlow_ref, xhigh_ref, ylow_ref, yhigh_ref, yjoin_ref, xown_ref, yown_ref,
    load_sem, store_sem, halo_send, halo_receive,
    xc_send, xc_receive, xv_send, xv_receive,
    yc_send, yc_receive, yv_send, yv_receive,
    yc2_send, yc2_receive, yv2_send, yv2_receive,
):
    nz, ny, nx, count_x, members, groups = sizes
    rows = nz * ny
    count_y = members * groups
    iy, ix = lax.axis_index("gy"), lax.axis_index("gx")
    group, member = iy // members, lax.rem(iy, members)

    def at_x(k):
        return (iy, k)

    def in_group(k):
        return (group * members + k, ix)

    def across(k):
        return (k * members + member, ix)

    loads = [
        pltpu.make_async_copy(source, target, load_sem.at[k])
        for k, (source, target) in enumerate(
            [
                (pressure_in, p_ref),
                (lateral_in.at[pl.ds(0, rows)], kx_ref),
                (lateral_in.at[pl.ds(rows, rows)], ky_ref),
                (vertical_in, kz_ref),
                (flux_in, f_ref),
                (memory_in, m_ref),
                (relax_in, relax_ref),
            ]
        )
    ]
    for load in loads:
        load.start()

    barrier = pltpu.get_barrier_semaphore()
    north, south = lax.rem(iy + 1, count_y), lax.rem(iy + count_y - 1, count_y)
    east, west = lax.rem(ix + 1, count_x), lax.rem(ix + count_x - 1, count_x)

    def greet(size, index, device):
        def turn(k, carry):
            pl.semaphore_signal(
                barrier,
                inc=1,
                device_id=device(lax.rem(index + k, size)),
                device_id_type=MESH,
            )
            return carry

        lax.fori_loop(1, size, turn, 0)

    for near in ((north, ix), (south, ix)):
        pl.semaphore_signal(barrier, inc=1, device_id=near, device_id_type=MESH)
    greet(count_x, ix, at_x)
    greet(members, member, in_group)
    greet(groups, group, across)

    lanes = lax.broadcasted_iota(jnp.int32, (rows, nx), 1)
    zero_plane = jnp.zeros((rows, nx), jnp.float32)

    for k in range(3):
        loads[k].wait()
    p = p_ref[...]
    kx = kx_ref[...]

    def strided(ref, y):
        return ref[pl.ds(y, nz, stride=ny), :]

    turned = jnp.transpose(jnp.where(lanes == 1, rolled_low(kx, 2), p))
    p_first, kx_last, p_last = turned[0:1], turned[1:2], turned[nx - 1 : nx]
    east_out[0:1] = p_last
    east_out[1:2] = kx_last
    west_out[...] = p_first
    north_out[0] = strided(p_ref, ny - 1)
    north_out[1] = strided(ky_ref, ny - 1)
    south_out[...] = strided(p_ref, 0)

    def halo(k, source, target, device):
        return pltpu.make_async_remote_copy(
            src_ref=source,
            dst_ref=target,
            send_sem=halo_send.at[k],
            recv_sem=halo_receive.at[k],
            device_id=device,
            device_id_type=MESH,
        )

    halos = [
        halo(0, east_out, west_in, (iy, east)),
        halo(1, west_out, east_in, (iy, west)),
        halo(2, north_out, south_in, (north, ix)),
        halo(3, south_out, north_in, (south, ix)),
    ]
    pl.semaphore_wait(barrier, 2 + count_x - 1 + members - 1 + groups - 1)
    for copy in halos:
        copy.start()

    half_y = 0.5 * jnp.stack([strided(ky_ref, y) for y in range(ny)])
    row = lax.broadcasted_iota(jnp.int32, half_y.shape, 0)
    vs, ws = factor(half_y, row, ny, major_low, major_high, y1_ref, y2_ref, yi_ref, True)
    vs_ref[...] = vs
    ws_ref[...] = ws
    yc_ref[member, 0] = vs[0]
    yc_ref[member, 1] = vs[ny - 1]
    yc_ref[member, 2] = ws[ny - 1]
    yc_ref[member, 3] = half_y[ny - 1]
    yc = Ring(yc_ref, (yc_send, yc_receive), members, member, in_group)
    yc.start()

    v, w = factor(0.5 * kx, lanes, nx, rolled_low, rolled_high, x1_ref, x2_ref, xi_ref, True)
    vt, wt = jnp.transpose(v), jnp.transpose(w)
    vt_ref[...] = vt
    wt_ref[...] = wt
    xc_ref[ix, 0:1] = vt[0:1]
    xc_ref[ix, 1:2] = vt[nx - 1 : nx]
    xc_ref[ix, 2:3] = wt[nx - 1 : nx]
    xc_ref[ix, 3:4] = 0.5 * kx_last
    xc = Ring(xc_ref, (xc_send, xc_receive), count_x, ix, at_x)
    xc.start()

    for k in range(3, 7):
        loads[k].wait()
    kz = kz_ref[...]
    planes = (nz, ny, nx)
    half_z = 0.5 * kz.reshape(planes)
    plane = lax.broadcasted_iota(jnp.int32, planes, 0)
    factor(half_z, plane, nz, major_low, major_high, z1_ref, z2_ref, zi_ref, False)
    p = p_ref[...]
    kx = kx_ref[...]
    explicit = kx * (jnp.where(lanes == nx - 1, zero_plane, rolled_high(p, 1)) - p)
    explicit -= jnp.where(
        lanes == 0, zero_plane, rolled_low(kx, 1) * (p - rolled_low(p, 1))
    )
    gap = jnp.zeros((ny, nx), jnp.float32)
    flow = kz * (jnp.concatenate([p[ny:], gap], axis=0) - p)
    explicit += flow - jnp.concatenate([gap, flow[: rows - ny]], axis=0)
    memory = m_ref[...].reshape(4, rows, nx)
    e_ref[...] = explicit + (f_ref[...] - (memory[0] + memory[1] + memory[2] + memory[3]))
    previous = None
    for y in range(ny):
        k_here, p_here = strided(ky_ref, y), strided(p_ref, y)
        p_next = strided(p_ref, y + 1) if y + 1 < ny else jnp.zeros_like(p_here)
        flow = k_here * (p_next - p_here)
        along = flow if previous is None else flow - previous
        e_ref[pl.ds(y, nz, stride=ny), :] = strided(e_ref, y) + along
        previous = flow
    weight = relax_ref[...]
    inverse = 1.0 / (1.0 + weight)
    iw_ref[...] = inverse
    wi_ref[...] = weight * inverse

    halos[2].wait_recv()
    halos[3].wait_recv()
    p_south = strided(p_ref, 0)
    k_north = strided(ky_ref, ny - 1)
    from_south = south_in[1] * (south_in[0] - p_south)
    from_south = jnp.where(iy == 0, jnp.zeros_like(from_south), from_south)
    from_north = k_north * north_in[...]
    from_north = jnp.where(iy == count_y - 1, jnp.zeros_like(from_north), from_north)
    e_ref[pl.ds(0, nz, stride=ny), :] = strided(e_ref, 0) + from_south
    e_ref[pl.ds(ny - 1, nz, stride=ny), :] = strided(e_ref, ny - 1) + from_north
    halos[0].wait_recv()
    halos[1].wait_recv()
    from_west = west_in[1:2] * (west_in[0:1] - west_out[...])
    from_west = jnp.where(ix == 0, jnp.zeros_like(from_west), from_west)
    from_east = east_out[1:2] * east_in[...]
    from_east = jnp.where(ix == count_x - 1, jnp.zeros_like(from_east), from_east)
    line = lax.broadcasted_iota(jnp.int32, (nx, rows), 0)
    edges = jnp.where(line == 0, from_west, jnp.where(line == nx - 1, from_east, 0.0))
    explicit = e_ref[...] + jnp.transpose(edges)

    step_z = reduce_lines(
        explicit.reshape(planes), nz, major_low, major_high, z1_ref, z2_ref, zi_ref
    )

    right = step_z.reshape(rows, nx)
    turned = jnp.transpose(right)
    xv_ref[ix, 0:1] = jnp.sum(vt_ref[...] * turned, axis=0, keepdims=True)
    xv_ref[ix, 1:2] = jnp.sum(wt_ref[...] * turned, axis=0, keepdims=True)
    xv = Ring(xv_ref, (xv_send, xv_receive), count_x, ix, at_x)
    xv.start()

    def saturated(d):
        return d * lax.rsqrt(1.0 + d * d)

    def relaxed(memory, d):
        target = saturated(d).reshape(1, nz, ny, nx)
        share = wi_ref[...].reshape(4, 1, ny, nx)
        return memory * iw_ref[...].reshape(4, 1, ny, nx) + share * target

    local_x = reduce_lines(right, nx, rolled_low, rolled_high, x1_ref, x2_ref, xi_ref)
    nm_ref[...] = relaxed(m_ref[...].reshape(4, nz, ny, nx), step_z).reshape(4 * rows, nx)
    e_ref[...] = local_x

    xc.arrive()

    def x_block(j):
        return tuple(xc_ref[j, k : k + 1] for k in range(4))

    own_x = tuple(xc_ref[ix, k : k + 1] for k in range(4))
    x_lower = [(j < ix, j) for j in range(count_x - 1)]
    x_upper = [(j > ix, j) for j in range(count_x - 1, 0, -1)]
    low_state, lows = below([(counts, x_block(j)) for counts, j in x_lower], own_x)
    g_above, highs = above([(counts, x_block(j)) for counts, j in x_upper], own_x)
    for n, pair in enumerate(lows):
        xlow_ref[n, 0:1], xlow_ref[n, 1:2] = pair
    for n, pair in enumerate(highs):
        xhigh_ref[n, 0:1], xhigh_ref[n, 1:2] = pair
    for n, part in enumerate(own_factors(own_x, low_state, g_above)):
        xown_ref[n : n + 1] = part

    yc.arrive()

    def y_block(j):
        return tuple(yc_ref[j, k] for k in range(4))

    made = []

    def combine(one, two):
        block, factors = join(one, two)
        made.append(factors)
        return block

    whole = join_all([y_block(j) for j in range(members)], combine)
    for n, factors in enumerate(made):
        for k in range(4):
            yjoin_ref[n, k] = factors[k]
    for k in range(4):
        yc2_ref[group, k] = whole[k]
    yc2 = Ring(yc2_ref, (yc2_send, yc2_receive), groups, group, across)
    yc2.start()

    xv.arrive()
    e_low = jnp.zeros_like(own_x[0])
    for n, (counts, j) in enumerate(x_lower):
        got = xv_ref[j, 1:2] - xlow_ref[n, 1:2] * xv_ref[j, 0:1] + xlow_ref[n, 0:1] * e_low
        e_low = jnp.where(counts, got, e_low)
    f_high = jnp.zeros_like(own_x[0])
    for n, (counts, j) in enumerate(x_upper):
        got = xv_ref[j, 0:1] + xhigh_ref[n, 1:2] * xv_ref[j, 1:2] + xhigh_ref[n, 0:1] * f_high
        f_high = jnp.where(counts, got, f_high)
    mine = (xv_ref[ix, 0:1], xv_ref[ix, 1:2])
    factors = tuple(xown_ref[n : n + 1] for n in range(8))
    lower_in, upper_in = inflow(own_x, factors, mine, e_low, f_high)
    step_x = e_ref[...] + jnp.transpose(vt_ref[...] * lower_in + wt_ref[...] * upper_in)

    e_ref[...] = step_x
    right = jnp.stack([strided(e_ref, y) for y in range(ny)])
    yv_ref[member, 0] = jnp.sum(vs_ref[...] * right, axis=0)
    yv_ref[member, 1] = jnp.sum(ws_ref[...] * right, axis=0)
    yv = Ring(yv_ref, (yv_send, yv_receive), members, member, in_group)
    yv.start()

    local_y = reduce_lines(right, ny, major_low, major_high, y1_ref, y2_ref, yi_ref)
    yi_ref[...] = local_y
    yc2.arrive()

    def y_group(j):
        return tuple(yc2_ref[j, k] for k in range(4))

    own_y = tuple(yc_ref[member, k] for k in range(4))
    lower_groups = [(j < group, j) for j in range(groups - 1)]
    upper_groups = [(j > group, j) for j in range(groups - 1, 0, -1)]
    lower_members = [(j < member, j) for j in range(members - 1)]
    upper_members = [(j > member, j) for j in range(members - 1, 0, -1)]
    low_state, lows = below(
        [(counts, y_group(j)) for counts, j in lower_groups]
        + [(counts, y_block(j)) for counts, j in lower_members],
        own_y,
    )
    g_above, highs = above(
        [(counts, y_group(j)) for counts, j in upper_groups]
        + [(counts, y_block(j)) for counts, j in upper_members],
        own_y,
    )
    for n, pair in enumerate(lows):
        ylow_ref[n, 0], ylow_ref[n, 1] = pair
    for n, pair in enumerate(highs):
        yhigh_ref[n, 0], yhigh_ref[n, 1] = pair
    for n, part in enumerate(own_factors(own_y, low_state, g_above)):
        yown_ref[n] = part

    yv.arrive()
    order = iter(range(members - 1))

    def combine_values(one, two):
        n = next(order)
        return join_values(tuple(yjoin_ref[n, k] for k in range(4)), one, two)

    whole = join_all([(yv_ref[j, 0], yv_ref[j, 1]) for j in range(members)], combine_values)
    yv2_ref[group, 0], yv2_ref[group, 1] = whole
    yv2 = Ring(yv2_ref, (yv2_send, yv2_receive), groups, group, across)
    yv2.start()

    memory = m_ref[...].reshape(4, rows, nx)
    partly = relaxed(nm_ref[...].reshape(4, nz, ny, nx), e_ref[...])
    partly = (partly * iw_ref[...].reshape(4, 1, ny, nx)).reshape(4, rows, nx)
    nm_ref[...] = partly.reshape(4 * rows, nx)
    moved = partly - memory
    nf_ref[...] = f_ref[...] - (moved[0] + moved[1] + moved[2] + moved[3])

    yv2.arrive()
    e_low = jnp.zeros_like(own_y[0])
    f_high = jnp.zeros_like(own_y[0])
    lower = [(counts, yv2_ref, j) for counts, j in lower_groups]
    lower += [(counts, yv_ref, j) for counts, j in lower_members]
    upper = [(counts, yv2_ref, j) for counts, j in upper_groups]
    upper += [(counts, yv_ref, j) for counts, j in upper_members]
    for n, (counts, ref, j) in enumerate(lower):
        got = ref[j, 1] - ylow_ref[n, 1] * ref[j, 0] + ylow_ref[n, 0] * e_low
        e_low = jnp.where(counts, got, e_low)
    for n, (counts, ref, j) in enumerate(upper):
        got = ref[j, 0] + yhigh_ref[n, 1] * ref[j, 1] + yhigh_ref[n, 0] * f_high
        f_high = jnp.where(counts, got, f_high)
    mine = (yv_ref[member, 0], yv_ref[member, 1])
    factors = tuple(yown_ref[n] for n in range(8))
    lower_in, upper_in = inflow(own_y, factors, mine, e_low, f_high)
    step_y = yi_ref[...] + vs_ref[...] * lower_in + ws_ref[...] * upper_in
    for y in range(ny):
        e_ref[pl.ds(y, nz, stride=ny), :] = step_y[y]
    step_y = e_ref[...]

    target = saturated(step_y)
    share = wi_ref[...].reshape(4, 1, ny, nx)
    nm = nm_ref[...].reshape(4, nz, ny, nx) + share * target.reshape(1, nz, ny, nx)
    nm_ref[...] = nm.reshape(4 * rows, nx)
    shares = (share[0] + share[1]) + (share[2] + share[3])
    nf_ref[...] = nf_ref[...] - (shares * target.reshape(planes)).reshape(rows, nx)
    np_ref[...] = p_ref[...] + step_y
    stores = [
        pltpu.make_async_copy(source, target, store_sem.at[k])
        for k, (source, target) in enumerate(
            [(nm_ref, memory_out), (nf_ref, flux_out), (np_ref, pressure_out)]
        )
    ]
    for store in stores:
        store.start()
    for copy in halos:
        copy.wait_send()
    for ring in (xc, yc, xv, yc2, yv, yv2):
        ring.finish()
    for store in stores:
        store.wait()


def local(mesh, pressure, fluid_flux, memory, lateral_faces, vertical_faces, relax_rates):
    nz, ny, nx = pressure.shape
    rows = nz * ny
    count_y, count_x = mesh.shape["gy"], mesh.shape["gx"]
    groups = 4 if count_y >= 16 else max(1, count_y // 2)
    members = count_y // groups
    sizes = (nz, ny, nx, count_x, members, groups)
    f32 = jnp.float32

    def vmem(*shape):
        return pltpu.VMEM(shape, f32)

    def dma(n):
        return pltpu.SemaphoreType.DMA((max(n, 1),))

    plane = (rows, nx)
    levels_x, levels_y, levels_z = (n.bit_length() - 1 for n in (nx, ny, nz))
    tile = (nz, nx)
    chain = members - 1 + groups - 1
    scratch = [
        vmem(*plane), vmem(*plane), vmem(4 * rows, nx), vmem(*plane), vmem(*plane),
        vmem(*plane), vmem(4 * ny, nx),
        vmem(*plane), vmem(*plane), vmem(4 * rows, nx),
        vmem(levels_x, *plane), vmem(levels_x, *plane), vmem(*plane),
        vmem(nx, rows), vmem(nx, rows),
        vmem(levels_y, ny, *tile), vmem(levels_y, ny, *tile), vmem(ny, *tile),
        vmem(ny, *tile), vmem(ny, *tile),
        vmem(levels_z, nz, ny, nx), vmem(levels_z, nz, ny, nx), vmem(nz, ny, nx),
        vmem(*plane), vmem(4 * ny, nx), vmem(4 * ny, nx),
        vmem(2, rows), vmem(1, rows), vmem(1, rows), vmem(2, rows),
        vmem(2, *tile), vmem(*tile), vmem(*tile), vmem(2, *tile),
        vmem(count_x, 4, rows), vmem(count_x, 2, rows),
        vmem(members, 4, *tile), vmem(members, 2, *tile),
        vmem(groups, 4, *tile), vmem(groups, 2, *tile),
        vmem(count_x, 2, rows), vmem(count_x, 2, rows),
        vmem(chain + 1, 2, *tile), vmem(chain + 1, 2, *tile),
        vmem(members, 4, *tile), vmem(8, rows), vmem(8, *tile),
        dma(7), dma(3), dma(4), dma(4),
    ]
    for n in (count_x, count_x, members, members, groups, groups):
        scratch += [dma(n - 1), dma(n - 1)]
    anywhere = pl.BlockSpec(memory_space=pl.ANY)
    outs = pl.pallas_call(
        partial(kernel, sizes),
        out_shape=(
            jax.ShapeDtypeStruct(plane, f32),
            jax.ShapeDtypeStruct(plane, f32),
            jax.ShapeDtypeStruct((4 * rows, nx), f32),
        ),
        in_specs=[anywhere] * 6,
        out_specs=(anywhere,) * 3,
        scratch_shapes=scratch,
        compiler_params=pltpu.CompilerParams(
            collective_id=0, has_side_effects=True, vmem_limit_bytes=60 << 20
        ),
        name="adi_step",
    )(
        pressure.reshape(plane),
        fluid_flux.reshape(plane),
        memory.reshape(4 * rows, nx),
        lateral_faces.reshape(2 * rows, nx),
        vertical_faces.reshape(plane),
        relax_rates.reshape(4 * ny, nx),
    )
    next_pressure, next_flux, next_memory = outs
    return (
        next_pressure.reshape(nz, ny, nx),
        next_flux.reshape(nz, ny, nx),
        next_memory.reshape(4, nz, ny, nx),
    )


def solution(mesh):
    in_specs = (
        P(None, "gy", "gx"),
        P(None, "gy", "gx"),
        P(None, None, "gy", "gx"),
        P(None, None, "gy", "gx"),
        P(None, "gy", "gx"),
        P(None, "gy", "gx"),
    )
    out_specs = (P(None, "gy", "gx"), P(None, "gy", "gx"), P(None, None, "gy", "gx"))
    return jax.shard_map(
        partial(local, mesh), mesh=mesh, in_specs=in_specs, out_specs=out_specs, check_vma=False
    )
```

```python
from functools import partial

import jax
import jax.numpy as jnp
from jax import lax
from jax.experimental import pallas as pl
from jax.experimental.pallas import tpu as pltpu
from jax.sharding import PartitionSpec as P

MESH = pl.DeviceIdType.MESH


def rolled_low(a, s):
    return pltpu.roll(a, s, axis=1)


def rolled_high(a, s):
    return pltpu.roll(a, a.shape[1] - s, axis=1)


def major_low(a, s):
    return jnp.concatenate([a[a.shape[0] - s :], a[: a.shape[0] - s]], axis=0)


def major_high(a, s):
    return jnp.concatenate([a[s:], a[:s]], axis=0)


def factor(half, position, n, low, high, k1_ref, k2_ref, inv_ref, ends):
    first, last = position == 0, position == n - 1
    zero = jnp.zeros_like(half)
    link = jnp.where(last, zero, half)
    main = 1.0 + half + jnp.where(first, zero, low(half, 1))
    columns = []
    if ends:
        one = jnp.ones_like(half)
        columns = [jnp.where(first, one, zero), jnp.where(last, one, zero)]
    s, level = 1, 0
    while s < n:
        inverse = 1.0 / main
        k2 = link * high(inverse, s)
        scaled = link * inverse
        k1 = low(scaled, s)
        k1_ref[level] = k1
        k2_ref[level] = k2
        columns = [v + k1 * low(v, s) + k2 * high(v, s) for v in columns]
        main = main - low(link * scaled, s) - link * k2
        link = k2 * high(link, s)
        s, level = 2 * s, level + 1
    inverse = 1.0 / main
    inv_ref[...] = inverse
    return [v * inverse for v in columns]


def reduce_lines(right, n, low, high, k1_ref, k2_ref, inv_ref):
    s, level = 1, 0
    while s < n:
        right = right + k1_ref[level] * low(right, s) + k2_ref[level] * high(right, s)
        s, level = 2 * s, level + 1
    return right * inv_ref[...]


def join(one, two):
    g1, c1, w1, h1 = one
    g2, c2, w2, h2 = two
    e1 = 1.0 - w1 * h1
    gh = g2 * h1
    d = 1.0 / (1.0 + gh * e1)
    up, down = c1 * h1 * d, c2 * h1 * d
    return g1 + up * gh * c1, up * c2, w2 - down * e1 * c2, h2


def join_all(blocks, combine):
    while len(blocks) > 1:
        blocks = [combine(blocks[k], blocks[k + 1]) for k in range(0, len(blocks), 2)]
    return blocks[0]


def below(blocks, state):
    top, bottom, h = state
    factors, states = [], []
    for counts, (gj, cj, wj, hj) in blocks:
        states.append((top, bottom, h))
        a = h * (bottom - top * h)
        new_bottom = bottom + gj * a
        new_top = wj * new_bottom - cj * cj * a
        t = cj / new_bottom
        factors.append((t * h * bottom, t * a))
        top = jnp.where(counts, new_top, top)
        bottom = jnp.where(counts, new_bottom, bottom)
        h = jnp.where(counts, hj, h)
    return (top, bottom, h), factors, states


def above(blocks, state):
    top, bottom = state
    factors, states = [], []
    for counts, (gj, cj, wj, hj) in blocks:
        states.append((top, bottom))
        ch = cj * hj
        new_bottom = bottom + top * (hj * (1.0 - wj * hj))
        new_top = gj * new_bottom + ch * ch * top
        t = ch / new_bottom
        factors.append((t * bottom, t * top * hj))
        top = jnp.where(counts, new_top, top)
        bottom = jnp.where(counts, new_bottom, bottom)
    return (top, bottom), factors, states


def own_factors(own, low_state, high_state):
    g, c, w, h = own
    top, bottom, h_low = low_state
    a = h_low * (bottom - top * h_low) / bottom
    gh = high_state[0] * h / high_state[1]
    p = h / (1.0 + gh)
    q = gh * p
    r1, r2, ca, cq = 1.0 + g * a, 1.0 - w * q, c * a, c * q
    inverse = 1.0 / (r1 * r2 + ca * cq)
    return (h_low, a, p, q, r1 * inverse, r2 * inverse, ca * inverse, cq * inverse)


def inflow(own, factors, mine, e_low, f_high):
    g, c, w, _ = own
    h_low, a, p, q, r1, r2, ca, cq = factors
    u, v = h_low * e_low, p * f_high
    s1 = mine[0] + g * u + c * v
    s2 = mine[1] + c * u + w * v
    return u - a * (r2 * s1 + cq * s2), v + q * (r1 * s2 - ca * s1)


class Ring:
    def __init__(self, buffer, sems, size, index, device, source=None):
        self.buffer, self.size, self.index, self.device = buffer, size, index, device
        self.send, self.receive = sems
        self.source = source or (lambda to: buffer.at[index])

    def copy(self, k):
        to = lax.rem(self.index + k, self.size)
        return pltpu.make_async_remote_copy(
            src_ref=self.source(to),
            dst_ref=self.buffer.at[self.index],
            send_sem=self.send.at[k - 1],
            recv_sem=self.receive.at[k - 1],
            device_id=self.device(to),
            device_id_type=MESH,
        )

    def each(self, act, start, stop):
        def turn(k, carry):
            act(self.copy(k))
            return carry

        if start < stop:
            lax.fori_loop(start, stop, turn, 0)

    def start(self, start=1, stop=None):
        self.each(lambda copy: copy.start(), start, stop or self.size)

    def arrive(self):
        self.each(lambda copy: copy.wait_recv(), 1, self.size)

    def finish(self):
        self.each(lambda copy: copy.wait_send(), 1, self.size)


def kernel(
    sizes,
    pressure_in, flux_in, memory_in, lateral_in, vertical_in, relax_in,
    step_out, flux_out, memory_out,
    p_ref, f_ref, m_ref, kx_ref, ky_ref, kz_ref, relax_ref,
    nf_ref, nm_ref,
    x1_ref, x2_ref, xi_ref, vt_ref, wt_ref,
    y1_ref, y2_ref, yi_ref, vs_ref, ws_ref,
    z1_ref, z2_ref, zi_ref,
    e_ref, iw_ref, wi_ref,
    east_out, west_out, east_in, west_in,
    north_out, south_out, north_in, south_in,
    xc_ref, xv_ref, yc_ref, yc2_ref, yv_ref, ys_ref,
    ylow_ref, yhigh_ref, yown_ref,
    load_sem, store_sem, halo_send, halo_receive, relay_sem,
    xc_send, xc_receive, xv_send, xv_receive,
    yc_send, yc_receive, yc2_send, yc2_receive, yv_send, yv_receive,
):
    nz, ny, nx, count_x, members, groups = sizes
    rows = nz * ny
    count_y = members * groups
    iy, ix = lax.axis_index("gy"), lax.axis_index("gx")
    group, member = iy // members, lax.rem(iy, members)
    reach = max(1, count_x // 4)
    near_stop = min(reach + 1, count_x)
    far_stop = max(near_stop, count_x - reach)

    def at_x(k):
        return (iy, k)

    def at_y(k):
        return (k, ix)

    def in_group(k):
        return (group * members + k, ix)

    def across(k):
        return (k * members + member, ix)

    loads = [
        pltpu.make_async_copy(source, target, load_sem.at[k])
        for k, (source, target) in enumerate(
            [
                (pressure_in, p_ref),
                (lateral_in.at[pl.ds(0, rows)], kx_ref),
                (lateral_in.at[pl.ds(rows, rows)], ky_ref),
                (vertical_in, kz_ref),
                (flux_in, f_ref),
                (memory_in, m_ref),
                (relax_in, relax_ref),
            ]
        )
    ]
    for load in loads:
        load.start()

    barrier = pltpu.get_barrier_semaphore()

    def greet(start, stop, size, index, device):
        def turn(k, carry):
            pl.semaphore_signal(
                barrier,
                inc=1,
                device_id=device(lax.rem(index + k, size)),
                device_id_type=MESH,
            )
            return carry

        if start < stop:
            lax.fori_loop(start, stop, turn, 0)

    greet(1, near_stop, count_x, ix, at_x)
    greet(far_stop, count_x, count_x, ix, at_x)
    greet(1, count_y, count_y, iy, at_y)
    greeted = near_stop - 1 + count_x - far_stop + count_y - 1

    lanes = lax.broadcasted_iota(jnp.int32, (rows, nx), 1)
    zero_plane = jnp.zeros((rows, nx), jnp.float32)
    planes = (nz, ny, nx)

    def strided(ref, y):
        return ref[pl.ds(y, nz, stride=ny), :]

    for k in range(3):
        loads[k].wait()
    p = p_ref[...]
    kx = kx_ref[...]
    turned = jnp.transpose(jnp.where(lanes == 1, rolled_low(kx, 2), p))
    p_first, kx_last, p_last = turned[0:1], turned[1:2], turned[nx - 1 : nx]
    east_out[0:1] = p_last
    east_out[1:2] = kx_last
    west_out[...] = p_first
    north_out[0] = strided(p_ref, ny - 1)
    north_out[1] = strided(ky_ref, ny - 1)
    south_out[...] = strided(p_ref, 0)

    v, w = factor(0.5 * kx, lanes, nx, rolled_low, rolled_high, x1_ref, x2_ref, xi_ref, True)
    vt, wt = jnp.transpose(v), jnp.transpose(w)
    vt_ref[...] = vt
    wt_ref[...] = wt
    xc_ref[ix, 0:1] = vt[0:1]
    xc_ref[ix, 1:2] = vt[nx - 1 : nx]
    xc_ref[ix, 2:3] = wt[nx - 1 : nx]
    xc_ref[ix, 3:4] = 0.5 * kx_last

    half_y = 0.5 * jnp.stack([strided(ky_ref, y) for y in range(ny)])
    row = lax.broadcasted_iota(jnp.int32, half_y.shape, 0)
    vs, ws = factor(half_y, row, ny, major_low, major_high, y1_ref, y2_ref, yi_ref, True)
    vs_ref[...] = vs
    ws_ref[...] = ws
    yc_ref[member, 0] = vs[0]
    yc_ref[member, 1] = vs[ny - 1]
    yc_ref[member, 2] = ws[ny - 1]
    yc_ref[member, 3] = half_y[ny - 1]

    for k in range(3, 7):
        loads[k].wait()
    kz = kz_ref[...]
    half_z = 0.5 * kz.reshape(planes)
    plane = lax.broadcasted_iota(jnp.int32, planes, 0)
    factor(half_z, plane, nz, major_low, major_high, z1_ref, z2_ref, zi_ref, False)
    p = p_ref[...]
    kx = kx_ref[...]
    explicit = kx * (jnp.where(lanes == nx - 1, zero_plane, rolled_high(p, 1)) - p)
    explicit -= jnp.where(
        lanes == 0, zero_plane, rolled_low(kx, 1) * (p - rolled_low(p, 1))
    )
    gap = jnp.zeros((ny, nx), jnp.float32)
    flow = kz * (jnp.concatenate([p[ny:], gap], axis=0) - p)
    explicit += flow - jnp.concatenate([gap, flow[: rows - ny]], axis=0)
    memory = m_ref[...].reshape(4, rows, nx)
    e_ref[...] = explicit + (f_ref[...] - (memory[0] + memory[1] + memory[2] + memory[3]))
    previous = None
    for y in range(ny):
        k_here, p_here = strided(ky_ref, y), strided(p_ref, y)
        p_next = strided(p_ref, y + 1) if y + 1 < ny else jnp.zeros_like(p_here)
        flow = k_here * (p_next - p_here)
        along = flow if previous is None else flow - previous
        e_ref[pl.ds(y, nz, stride=ny), :] = strided(e_ref, y) + along
        previous = flow
    weight = relax_ref[...]
    inverse = 1.0 / (1.0 + weight)
    iw_ref[...] = inverse
    wi_ref[...] = weight * inverse

    north, south = lax.rem(iy + 1, count_y), lax.rem(iy + count_y - 1, count_y)
    east, west = lax.rem(ix + 1, count_x), lax.rem(ix + count_x - 1, count_x)

    def halo(k, source, target, device):
        return pltpu.make_async_remote_copy(
            src_ref=source,
            dst_ref=target,
            send_sem=halo_send.at[k],
            recv_sem=halo_receive.at[k],
            device_id=device,
            device_id_type=MESH,
        )

    halos = [
        halo(0, east_out, west_in, (iy, east)),
        halo(1, west_out, east_in, (iy, west)),
        halo(2, north_out, south_in, (north, ix)),
        halo(3, south_out, north_in, (south, ix)),
    ]
    xc = Ring(xc_ref, (xc_send, xc_receive), count_x, ix, at_x)
    xv = Ring(xv_ref, (xv_send, xv_receive), count_x, ix, at_x)
    yc = Ring(yc_ref, (yc_send, yc_receive), members, member, in_group)
    yc2 = Ring(yc2_ref, (yc2_send, yc2_receive), groups, group, across)

    pl.semaphore_wait(barrier, greeted)
    for copy in halos:
        copy.start()
    if near_stop < far_stop:
        for far in (lax.rem(ix + reach, count_x), lax.rem(ix + count_x - reach, count_x)):
            pl.semaphore_signal(relay_sem, inc=1, device_id=(iy, far), device_id_type=MESH)
    xc.start(1, near_stop)
    xc.start(far_stop, count_x)
    yc.start()

    halos[2].wait_recv()
    halos[3].wait_recv()
    p_south = strided(p_ref, 0)
    k_north = strided(ky_ref, ny - 1)
    from_south = south_in[1] * (south_in[0] - p_south)
    from_south = jnp.where(iy == 0, jnp.zeros_like(from_south), from_south)
    from_north = k_north * north_in[...]
    from_north = jnp.where(iy == count_y - 1, jnp.zeros_like(from_north), from_north)
    e_ref[pl.ds(0, nz, stride=ny), :] = strided(e_ref, 0) + from_south
    e_ref[pl.ds(ny - 1, nz, stride=ny), :] = strided(e_ref, ny - 1) + from_north
    halos[0].wait_recv()
    halos[1].wait_recv()
    from_west = west_in[1:2] * (west_in[0:1] - west_out[...])
    from_west = jnp.where(ix == 0, jnp.zeros_like(from_west), from_west)
    from_east = east_out[1:2] * east_in[...]
    from_east = jnp.where(ix == count_x - 1, jnp.zeros_like(from_east), from_east)
    line = lax.broadcasted_iota(jnp.int32, (nx, rows), 0)
    edges = jnp.where(line == 0, from_west, jnp.where(line == nx - 1, from_east, 0.0))
    explicit = e_ref[...] + jnp.transpose(edges)

    step_z = reduce_lines(
        explicit.reshape(planes), nz, major_low, major_high, z1_ref, z2_ref, zi_ref
    )

    right = step_z.reshape(rows, nx)
    turned = jnp.transpose(right)
    xv_ref[ix, 0:1] = jnp.sum(vt_ref[...] * turned, axis=0, keepdims=True)
    xv_ref[ix, 1:2] = jnp.sum(wt_ref[...] * turned, axis=0, keepdims=True)
    xv.start(1, near_stop)
    xv.start(far_stop, count_x)
    if near_stop < far_stop:
        pl.semaphore_wait(relay_sem, 2)
        xc.start(near_stop, far_stop)
        xv.start(near_stop, far_stop)

    yc.arrive()

    def y_block(j):
        return tuple(yc_ref[j, k] for k in range(4))

    whole = join_all([y_block(j) for j in range(members)], join)
    for k in range(4):
        yc2_ref[group, k] = whole[k]
    yc2.start()

    def saturated(d):
        return d * lax.rsqrt(1.0 + d * d)

    def relaxed(memory, d):
        target = saturated(d).reshape(1, nz, ny, nx)
        share = wi_ref[...].reshape(4, 1, ny, nx)
        return memory * iw_ref[...].reshape(4, 1, ny, nx) + share * target

    local_x = reduce_lines(right, nx, rolled_low, rolled_high, x1_ref, x2_ref, xi_ref)
    nm_ref[...] = relaxed(m_ref[...].reshape(4, nz, ny, nx), step_z).reshape(4 * rows, nx)
    e_ref[...] = local_x

    yc2.arrive()

    def y_group(j):
        return tuple(yc2_ref[j, k] for k in range(4))

    own_y = tuple(yc_ref[member, k] for k in range(4))
    zero, one = jnp.zeros_like(own_y[0]), jnp.ones_like(own_y[0])
    state, lows, _ = below([(j < group, y_group(j)) for j in range(groups - 1)], (zero, one, zero))
    _, low_members, low_states = below([(True, y_block(j)) for j in range(members)], state)
    uppers = list(range(groups - 1, 0, -1))
    state, highs, _ = above([(j > group, y_group(j)) for j in uppers], (zero, one))
    downward = list(range(members - 1, -1, -1))
    _, high_members, high_states = above([(True, y_block(j)) for j in downward], state)
    high_members, high_states = high_members[::-1], high_states[::-1]
    low_state, high_state = low_states[0], high_states[0]
    low_own, high_own = low_members[0], high_members[0]
    for j in range(1, members):
        low_state, high_state, low_own, high_own = jax.tree.map(
            lambda new, old: jnp.where(member == j, new, old),
            (low_states[j], high_states[j], low_members[j], high_members[j]),
            (low_state, high_state, low_own, high_own),
        )
    past_above, past_below = one, one
    for j in range(members):
        past_above = jnp.where(j > member, past_above * low_members[j][0], past_above)
        past_below = jnp.where(j < member, past_below * high_members[j][0], past_below)
    for n in range(members):
        ylow_ref[groups + n] = low_members[n][0]
        yhigh_ref[groups + n] = high_members[n][0]
    for n in range(groups - 1):
        ylow_ref[n] = lows[n][0]
        yhigh_ref[n] = highs[n][0]
    own_parts = own_factors(own_y, low_state, high_state)
    own_parts += (low_own[1], high_own[1], past_above, past_below)
    for n, part in enumerate(own_parts):
        yown_ref[n] = part

    xc.arrive()

    def x_block(j):
        return tuple(xc_ref[j, k : k + 1] for k in range(4))

    own_x = tuple(xc_ref[ix, k : k + 1] for k in range(4))
    zero, one = jnp.zeros_like(own_x[0]), jnp.ones_like(own_x[0])
    x_lower = [(j < ix, j) for j in range(count_x - 1)]
    x_upper = [(j > ix, j) for j in range(count_x - 1, 0, -1)]
    low_state, lows, _ = below([(c, x_block(j)) for c, j in x_lower], (zero, one, zero))
    high_state, highs, _ = above([(c, x_block(j)) for c, j in x_upper], (zero, one))
    factors = own_factors(own_x, low_state, high_state)

    xv.arrive()
    e_low, f_high = zero, zero
    for (counts, j), (kappa, eps) in zip(x_lower, lows):
        got = xv_ref[j, 1:2] - eps * xv_ref[j, 0:1] + kappa * e_low
        e_low = jnp.where(counts, got, e_low)
    for (counts, j), (kappa, eps) in zip(x_upper, highs):
        got = xv_ref[j, 0:1] + eps * xv_ref[j, 1:2] + kappa * f_high
        f_high = jnp.where(counts, got, f_high)
    mine = (xv_ref[ix, 0:1], xv_ref[ix, 1:2])
    lower_in, upper_in = inflow(own_x, factors, mine, e_low, f_high)
    step_x = e_ref[...] + jnp.transpose(vt_ref[...] * lower_in + wt_ref[...] * upper_in)

    e_ref[...] = step_x
    right = jnp.stack([strided(e_ref, y) for y in range(ny)])
    first = jnp.sum(vs_ref[...] * right, axis=0)
    last = jnp.sum(ws_ref[...] * right, axis=0)
    upward = last - yown_ref[8] * first
    downwards = first + yown_ref[9] * last
    ys_ref[0], ys_ref[1] = downwards, upward
    ys_ref[2], ys_ref[3] = downwards * yown_ref[11], upward * yown_ref[10]
    yv_ref[iy] = jnp.zeros_like(first)

    def toward(to):
        outside = jnp.where(to // members == group, 0, 2)
        return ys_ref.at[outside + jnp.where(to > iy, 1, 0)]

    yv = Ring(yv_ref, (yv_send, yv_receive), count_y, iy, at_y, toward)
    yv.start()

    yi_ref[...] = reduce_lines(right, ny, major_low, major_high, y1_ref, y2_ref, yi_ref)
    memory = m_ref[...].reshape(4, rows, nx)
    partly = relaxed(nm_ref[...].reshape(4, nz, ny, nx), e_ref[...])
    partly = (partly * iw_ref[...].reshape(4, 1, ny, nx)).reshape(4, rows, nx)
    nm_ref[...] = partly.reshape(4 * rows, nx)
    moved = partly - memory
    nf_ref[...] = f_ref[...] - (moved[0] + moved[1] + moved[2] + moved[3])
    stores = [
        pltpu.make_async_copy(nm_ref, memory_out, store_sem.at[0]),
        pltpu.make_async_copy(nf_ref, flux_out, store_sem.at[1]),
    ]
    for store in stores:
        store.start()

    yv.arrive()
    e_low, f_high = jnp.zeros_like(first), jnp.zeros_like(first)
    sums = []
    for j in range(groups):
        parts = [yv_ref[j * members + k] for k in range(members)]
        sums.append(join_all(parts, lambda a, b: a + b))
    for j in range(groups - 1):
        e_low = jnp.where(j < group, sums[j] + ylow_ref[j] * e_low, e_low)
    for n, j in enumerate(uppers):
        f_high = jnp.where(j > group, sums[j] + yhigh_ref[n] * f_high, f_high)
    for j in range(members - 1):
        got = yv_ref[group * members + j] + ylow_ref[groups + j] * e_low
        e_low = jnp.where(j < member, got, e_low)
    for j in downward[:-1]:
        got = yv_ref[group * members + j] + yhigh_ref[groups + j] * f_high
        f_high = jnp.where(j > member, got, f_high)
    own_y = tuple(yc_ref[member, k] for k in range(4))
    factors = tuple(yown_ref[n] for n in range(8))
    lower_in, upper_in = inflow(own_y, factors, (first, last), e_low, f_high)
    step_y = yi_ref[...] + vs_ref[...] * lower_in + ws_ref[...] * upper_in
    for y in range(ny):
        e_ref[pl.ds(y, nz, stride=ny), :] = step_y[y]
    final = pltpu.make_async_copy(e_ref, step_out, store_sem.at[2])
    final.start()
    for copy in halos:
        copy.wait_send()
    for ring in (xc, yc, xv, yc2, yv):
        ring.finish()
    for store in stores:
        store.wait()
    final.wait()


def last_relaxation(
    sizes, step_in, flux_in, memory_in, pressure_in, relax_in,
    pressure_out, flux_out, memory_out,
    s_ref, f_ref, m_ref, p_ref, r_ref, load_sem, store_sem,
):
    nz, ny, nx = sizes
    rows = nz * ny
    pairs = [
        (step_in, s_ref), (pressure_in, p_ref), (relax_in, r_ref),
        (memory_in, m_ref), (flux_in, f_ref),
    ]
    loads = [pltpu.make_async_copy(a, b, load_sem.at[k]) for k, (a, b) in enumerate(pairs)]
    for load in loads:
        load.start()
    pairs = [(p_ref, pressure_out), (m_ref, memory_out), (f_ref, flux_out)]
    stores = [pltpu.make_async_copy(a, b, store_sem.at[k]) for k, (a, b) in enumerate(pairs)]
    loads[0].wait()
    loads[1].wait()
    step = s_ref[...]
    p_ref[...] = p_ref[...] + step
    stores[0].start()
    loads[2].wait()
    target = (step * lax.rsqrt(1.0 + step * step)).reshape(nz, ny, nx)
    weight = r_ref[...].reshape(4, 1, ny, nx)
    share = weight / (1.0 + weight)
    loads[3].wait()
    memory = m_ref[...].reshape(4, nz, ny, nx) + share * target[None]
    m_ref[...] = memory.reshape(4 * rows, nx)
    stores[1].start()
    loads[4].wait()
    shares = (share[0] + share[1]) + (share[2] + share[3])
    f_ref[...] = f_ref[...] - (shares * target).reshape(rows, nx)
    stores[2].start()
    for store in stores:
        store.wait()


def local(mesh, pressure, fluid_flux, memory, lateral_faces, vertical_faces, relax_rates):
    nz, ny, nx = pressure.shape
    rows = nz * ny
    count_y, count_x = mesh.shape["gy"], mesh.shape["gx"]
    groups = 4 if count_y >= 16 else max(1, count_y // 2)
    members = count_y // groups
    sizes = (nz, ny, nx, count_x, members, groups)
    f32 = jnp.float32

    def vmem(*shape):
        return pltpu.VMEM(shape, f32)

    def dma(n):
        return pltpu.SemaphoreType.DMA((max(n, 1),))

    plane = (rows, nx)
    levels_x, levels_y, levels_z = (n.bit_length() - 1 for n in (nx, ny, nz))
    tile = (nz, nx)
    scratch = [
        vmem(*plane), vmem(*plane), vmem(4 * rows, nx), vmem(*plane), vmem(*plane),
        vmem(*plane), vmem(4 * ny, nx),
        vmem(*plane), vmem(4 * rows, nx),
        vmem(levels_x, *plane), vmem(levels_x, *plane), vmem(*plane),
        vmem(nx, rows), vmem(nx, rows),
        vmem(levels_y, ny, *tile), vmem(levels_y, ny, *tile), vmem(ny, *tile),
        vmem(ny, *tile), vmem(ny, *tile),
        vmem(levels_z, nz, ny, nx), vmem(levels_z, nz, ny, nx), vmem(nz, ny, nx),
        vmem(*plane), vmem(4 * ny, nx), vmem(4 * ny, nx),
        vmem(2, rows), vmem(1, rows), vmem(1, rows), vmem(2, rows),
        vmem(2, *tile), vmem(*tile), vmem(*tile), vmem(2, *tile),
        vmem(count_x, 4, rows), vmem(count_x, 2, rows),
        vmem(members, 4, *tile), vmem(groups, 4, *tile), vmem(count_y, *tile), vmem(4, *tile),
        vmem(members + groups, *tile), vmem(members + groups, *tile), vmem(12, *tile),
        dma(7), dma(3), dma(4), dma(4), pltpu.SemaphoreType.REGULAR,
    ]
    for n in (count_x, count_x, members, groups, count_y):
        scratch += [dma(n - 1), dma(n - 1)]
    anywhere = pl.BlockSpec(memory_space=pl.ANY)
    outs = pl.pallas_call(
        partial(kernel, sizes),
        out_shape=(
            jax.ShapeDtypeStruct(plane, f32),
            jax.ShapeDtypeStruct(plane, f32),
            jax.ShapeDtypeStruct((4 * rows, nx), f32),
        ),
        in_specs=[anywhere] * 6,
        out_specs=(anywhere,) * 3,
        scratch_shapes=scratch,
        compiler_params=pltpu.CompilerParams(
            collective_id=0, has_side_effects=True, vmem_limit_bytes=60 << 20
        ),
        name="adi_step",
    )(
        pressure.reshape(plane),
        fluid_flux.reshape(plane),
        memory.reshape(4 * rows, nx),
        lateral_faces.reshape(2 * rows, nx),
        vertical_faces.reshape(plane),
        relax_rates.reshape(4 * ny, nx),
    )
    step, flux, memory = outs
    next_pressure, next_flux, next_memory = pl.pallas_call(
        partial(last_relaxation, (nz, ny, nx)),
        out_shape=(
            jax.ShapeDtypeStruct(plane, f32),
            jax.ShapeDtypeStruct(plane, f32),
            jax.ShapeDtypeStruct((4 * rows, nx), f32),
        ),
        in_specs=[anywhere] * 5,
        out_specs=(anywhere,) * 3,
        scratch_shapes=[
            vmem(*plane), vmem(*plane), vmem(4 * rows, nx), vmem(*plane), vmem(4 * ny, nx),
            dma(5), dma(3),
        ],
        compiler_params=pltpu.CompilerParams(vmem_limit_bytes=60 << 20),
        name="last_relaxation",
    )(step, flux, memory, pressure.reshape(plane), relax_rates.reshape(4 * ny, nx))
    return (
        next_pressure.reshape(nz, ny, nx),
        next_flux.reshape(nz, ny, nx),
        next_memory.reshape(4, nz, ny, nx),
    )


def solution(mesh):
    in_specs = (
        P(None, "gy", "gx"),
        P(None, "gy", "gx"),
        P(None, None, "gy", "gx"),
        P(None, None, "gy", "gx"),
        P(None, "gy", "gx"),
        P(None, "gy", "gx"),
    )
    out_specs = (P(None, "gy", "gx"), P(None, "gy", "gx"), P(None, None, "gy", "gx"))
    return jax.shard_map(
        partial(local, mesh), mesh=mesh, in_specs=in_specs, out_specs=out_specs, check_vma=False
    )
```

```python
from functools import partial

import jax
import jax.numpy as jnp
from jax import lax
from jax.experimental import pallas as pl
from jax.experimental.pallas import tpu as pltpu
from jax.sharding import PartitionSpec as P

MESH = pl.DeviceIdType.MESH


def rolled_low(a, s):
    return pltpu.roll(a, s, axis=1)


def rolled_high(a, s):
    return pltpu.roll(a, a.shape[1] - s, axis=1)


def major_low(a, s):
    return jnp.concatenate([a[a.shape[0] - s :], a[: a.shape[0] - s]], axis=0)


def major_high(a, s):
    return jnp.concatenate([a[s:], a[:s]], axis=0)


def factor(half, position, n, low, high, k1_ref, k2_ref, inv_ref, ends):
    first, last = position == 0, position == n - 1
    zero = jnp.zeros_like(half)
    link = jnp.where(last, zero, half)
    main = 1.0 + half + jnp.where(first, zero, low(half, 1))
    columns = []
    if ends:
        one = jnp.ones_like(half)
        columns = [jnp.where(first, one, zero), jnp.where(last, one, zero)]
    s, level = 1, 0
    while s < n:
        inverse = 1.0 / main
        k2 = link * high(inverse, s)
        scaled = link * inverse
        k1 = low(scaled, s)
        k1_ref[level] = k1
        k2_ref[level] = k2
        columns = [v + k1 * low(v, s) + k2 * high(v, s) for v in columns]
        main = main - low(link * scaled, s) - link * k2
        link = k2 * high(link, s)
        s, level = 2 * s, level + 1
    inverse = 1.0 / main
    inv_ref[...] = inverse
    return [v * inverse for v in columns]


def reduce_lines(right, n, low, high, k1_ref, k2_ref, inv_ref):
    s, level = 1, 0
    while s < n:
        right = right + k1_ref[level] * low(right, s) + k2_ref[level] * high(right, s)
        s, level = 2 * s, level + 1
    return right * inv_ref[...]


def join(one, two):
    g1, c1, w1, h1 = one
    g2, c2, w2, h2 = two
    e1 = 1.0 - w1 * h1
    gh = g2 * h1
    d = 1.0 / (1.0 + gh * e1)
    up, down = c1 * h1 * d, c2 * h1 * d
    return g1 + up * gh * c1, up * c2, w2 - down * e1 * c2, h2


def join_all(blocks, combine):
    while len(blocks) > 1:
        blocks = [combine(blocks[k], blocks[k + 1]) for k in range(0, len(blocks), 2)]
    return blocks[0]


def below(blocks, state):
    top, bottom, h = state
    factors, states = [], []
    for counts, (gj, cj, wj, hj) in blocks:
        states.append((top, bottom, h))
        a = h * (bottom - top * h)
        new_bottom = bottom + gj * a
        new_top = wj * new_bottom - cj * cj * a
        t = cj / new_bottom
        factors.append((t * h * bottom, t * a))
        top = jnp.where(counts, new_top, top)
        bottom = jnp.where(counts, new_bottom, bottom)
        h = jnp.where(counts, hj, h)
    return (top, bottom, h), factors, states


def above(blocks, state):
    top, bottom = state
    factors, states = [], []
    for counts, (gj, cj, wj, hj) in blocks:
        states.append((top, bottom))
        ch = cj * hj
        new_bottom = bottom + top * (hj * (1.0 - wj * hj))
        new_top = gj * new_bottom + ch * ch * top
        t = ch / new_bottom
        factors.append((t * bottom, t * top * hj))
        top = jnp.where(counts, new_top, top)
        bottom = jnp.where(counts, new_bottom, bottom)
    return (top, bottom), factors, states


def below_fractions(blocks, state):
    top, bottom, h = state
    factors = []
    for counts, (gj, cj, wj, hj) in blocks:
        a = h * (bottom - top * h)
        new_bottom = bottom + gj * a
        mixed = cj * a
        factors.append((new_bottom, cj * h, mixed))
        new_top = wj * new_bottom - cj * mixed
        top = jnp.where(counts, new_top, top)
        bottom = jnp.where(counts, new_bottom, bottom)
        h = jnp.where(counts, hj, h)
    return (top, bottom, h), factors


def above_fractions(blocks, state):
    top, bottom = state
    factors = []
    for counts, (gj, cj, wj, hj) in blocks:
        ch = cj * hj
        new_bottom = bottom + top * (hj * (1.0 - wj * hj))
        factors.append((new_bottom, ch, ch * hj * top))
        new_top = gj * new_bottom + ch * ch * top
        top = jnp.where(counts, new_top, top)
        bottom = jnp.where(counts, new_bottom, bottom)
    return (top, bottom), factors


def own_factors(own, low_state, high_state):
    g, c, w, h = own
    top, bottom, h_low = low_state
    a = h_low * (bottom - top * h_low) / bottom
    gh = high_state[0] * h / high_state[1]
    p = h / (1.0 + gh)
    q = gh * p
    r1, r2, ca, cq = 1.0 + g * a, 1.0 - w * q, c * a, c * q
    inverse = 1.0 / (r1 * r2 + ca * cq)
    return (h_low, a, p, q, r1 * inverse, r2 * inverse, ca * inverse, cq * inverse)


def inflow(own, factors, mine, e_low, f_high):
    g, c, w, _ = own
    h_low, a, p, q, r1, r2, ca, cq = factors
    u, v = h_low * e_low, p * f_high
    s1 = mine[0] + g * u + c * v
    s2 = mine[1] + c * u + w * v
    return u - a * (r2 * s1 + cq * s2), v + q * (r1 * s2 - ca * s1)


class Steps:
    def __init__(self, sizes, index):
        self.sizes, self.index = sizes, index
        self.count = 1
        for size in sizes:
            self.count *= size

    def split(self, number):
        digits = []
        for size in self.sizes[::-1]:
            digits.append(number % size)
            number = number // size
        return digits[::-1]

    def to(self, k):
        place = 0
        for size, at, step in zip(self.sizes, self.split(self.index), self.split(k)):
            place = place * size + (lax.rem(at + step, size) if step else at)
        return place

    def hops(self, k):
        return sum(min(step, size - step) for size, step in zip(self.sizes, self.split(k)))

    def far_first(self, least=1, most=99):
        steps = [k for k in range(1, self.count) if least <= self.hops(k) <= most]
        return sorted(steps, key=lambda k: -self.hops(k))


class Ring:
    def __init__(self, buffer, sems, steps, device, source=None):
        self.buffer, self.steps, self.device = buffer, steps, device
        self.send, self.receive = sems
        self.source = source or (lambda to: buffer.at[steps.index])

    def start(self, least=1, most=99):
        for k in self.steps.far_first(least, most):
            to = self.steps.to(k)
            pltpu.make_async_remote_copy(
                src_ref=self.source(to),
                dst_ref=self.buffer.at[self.steps.index],
                send_sem=self.send,
                recv_sem=self.receive,
                device_id=self.device(to),
                device_id_type=MESH,
            ).start()

    def all(self):
        every = self.buffer.at[pl.ds(0, self.steps.count - 1)]
        return pltpu.make_async_remote_copy(
            src_ref=every,
            dst_ref=every,
            send_sem=self.send,
            recv_sem=self.receive,
            device_id=self.device(self.steps.to(1)),
            device_id_type=MESH,
        )

    def arrive(self):
        self.all().wait_recv()

    def finish(self):
        self.all().wait_send()


def kernel(
    sizes,
    pressure_in, flux_in, memory_in, lateral_in, vertical_in, relax_in,
    step_out, flux_out, memory_out,
    p_ref, f_ref, m_ref, kx_ref, ky_ref, kz_ref, relax_ref,
    nf_ref, nm_ref,
    x1_ref, x2_ref, xi_ref, vt_ref, wt_ref,
    y1_ref, y2_ref, yi_ref, vs_ref, ws_ref,
    z1_ref, z2_ref, zi_ref,
    e_ref, iw_ref, wi_ref,
    east_out, west_out, east_in, west_in,
    north_out, south_out, north_in, south_in,
    xc_ref, xv_ref, yc_ref, yc2_ref, yv_ref, ys_ref,
    ylow_ref, yhigh_ref, yown_ref,
    load_sem, store_sem, halo_send, halo_receive, relay_sem,
    xc_send, xc_receive, xv_send, xv_receive,
    yc_send, yc_receive, yc2_send, yc2_receive, yv_send, yv_receive,
):
    nz, ny, nx, count_x, members, groups = sizes
    rows = nz * ny
    count_y = members * groups
    iy, ix = lax.axis_index("gy"), lax.axis_index("gx")
    group, member = iy // members, lax.rem(iy, members)
    reach = max(1, count_x // 4)
    beyond = count_x // 2 > reach
    along_x = Steps((count_x,), ix)
    along_y = Steps((4, 4, 2) if count_y == 32 else (count_y,), iy)
    inside = Steps((members // 2, 2), member)
    between = Steps((groups,), group)

    def at_x(k):
        return (iy, k)

    def at_y(k):
        return (k, ix)

    def in_group(k):
        return (group * members + k, ix)

    def across(k):
        return (k * members + member, ix)

    loads = [
        pltpu.make_async_copy(source, target, load_sem.at[k])
        for k, (source, target) in enumerate(
            [
                (pressure_in, p_ref),
                (lateral_in.at[pl.ds(0, rows)], kx_ref),
                (lateral_in.at[pl.ds(rows, rows)], ky_ref),
                (vertical_in, kz_ref),
                (flux_in, f_ref),
                (memory_in, m_ref),
                (relax_in, relax_ref),
            ]
        )
    ]
    for load in loads:
        load.start()

    barrier = pltpu.get_barrier_semaphore()

    greeted = 0
    for steps, device, most in ((along_x, at_x, reach), (along_y, at_y, 99)):
        for k in steps.far_first(1, most):
            pl.semaphore_signal(
                barrier, inc=1, device_id=device(steps.to(k)), device_id_type=MESH
            )
            greeted += 1

    lanes = lax.broadcasted_iota(jnp.int32, (rows, nx), 1)
    zero_plane = jnp.zeros((rows, nx), jnp.float32)
    planes = (nz, ny, nx)

    def strided(ref, y):
        return ref[pl.ds(y, nz, stride=ny), :]

    for k in range(3):
        loads[k].wait()
    p = p_ref[...]
    kx = kx_ref[...]
    turned = jnp.transpose(jnp.where(lanes == 1, rolled_low(kx, 2), p))
    p_first, kx_last, p_last = turned[0:1], turned[1:2], turned[nx - 1 : nx]
    east_out[0:1] = p_last
    east_out[1:2] = kx_last
    west_out[...] = p_first
    north_out[0] = strided(p_ref, ny - 1)
    north_out[1] = strided(ky_ref, ny - 1)
    south_out[...] = strided(p_ref, 0)

    v, w = factor(0.5 * kx, lanes, nx, rolled_low, rolled_high, x1_ref, x2_ref, xi_ref, True)
    vt, wt = jnp.transpose(v), jnp.transpose(w)
    vt_ref[...] = vt
    wt_ref[...] = wt
    xc_ref[ix, 0:1] = vt[0:1]
    xc_ref[ix, 1:2] = vt[nx - 1 : nx]
    xc_ref[ix, 2:3] = wt[nx - 1 : nx]
    xc_ref[ix, 3:4] = 0.5 * kx_last

    half_y = 0.5 * jnp.stack([strided(ky_ref, y) for y in range(ny)])
    row = lax.broadcasted_iota(jnp.int32, half_y.shape, 0)
    vs, ws = factor(half_y, row, ny, major_low, major_high, y1_ref, y2_ref, yi_ref, True)
    vs_ref[...] = vs
    ws_ref[...] = ws
    yc_ref[member, 0] = vs[0]
    yc_ref[member, 1] = vs[ny - 1]
    yc_ref[member, 2] = ws[ny - 1]
    yc_ref[member, 3] = half_y[ny - 1]

    for k in range(3, 7):
        loads[k].wait()
    kz = kz_ref[...]
    half_z = 0.5 * kz.reshape(planes)
    plane = lax.broadcasted_iota(jnp.int32, planes, 0)
    factor(half_z, plane, nz, major_low, major_high, z1_ref, z2_ref, zi_ref, False)
    p = p_ref[...]
    kx = kx_ref[...]
    explicit = kx * (jnp.where(lanes == nx - 1, zero_plane, rolled_high(p, 1)) - p)
    explicit -= jnp.where(
        lanes == 0, zero_plane, rolled_low(kx, 1) * (p - rolled_low(p, 1))
    )
    gap = jnp.zeros((ny, nx), jnp.float32)
    flow = kz * (jnp.concatenate([p[ny:], gap], axis=0) - p)
    explicit += flow - jnp.concatenate([gap, flow[: rows - ny]], axis=0)
    memory = m_ref[...].reshape(4, rows, nx)
    e_ref[...] = explicit + (f_ref[...] - (memory[0] + memory[1] + memory[2] + memory[3]))
    previous = None
    for y in range(ny):
        k_here, p_here = strided(ky_ref, y), strided(p_ref, y)
        p_next = strided(p_ref, y + 1) if y + 1 < ny else jnp.zeros_like(p_here)
        flow = k_here * (p_next - p_here)
        along = flow if previous is None else flow - previous
        e_ref[pl.ds(y, nz, stride=ny), :] = strided(e_ref, y) + along
        previous = flow
    weight = relax_ref[...]
    inverse = 1.0 / (1.0 + weight)
    iw_ref[...] = inverse
    wi_ref[...] = weight * inverse

    north, south = lax.rem(iy + 1, count_y), lax.rem(iy + count_y - 1, count_y)
    east, west = lax.rem(ix + 1, count_x), lax.rem(ix + count_x - 1, count_x)

    def halo(k, source, target, device):
        return pltpu.make_async_remote_copy(
            src_ref=source,
            dst_ref=target,
            send_sem=halo_send.at[k],
            recv_sem=halo_receive.at[k],
            device_id=device,
            device_id_type=MESH,
        )

    halos = [
        halo(0, east_out, west_in, (iy, east)),
        halo(1, west_out, east_in, (iy, west)),
        halo(2, north_out, south_in, (north, ix)),
        halo(3, south_out, north_in, (south, ix)),
    ]
    xc = Ring(xc_ref, (xc_send, xc_receive), along_x, at_x)
    xv = Ring(xv_ref, (xv_send, xv_receive), along_x, at_x)
    yc = Ring(yc_ref, (yc_send, yc_receive), inside, in_group)
    yc2 = Ring(yc2_ref, (yc2_send, yc2_receive), between, across)

    pl.semaphore_wait(barrier, greeted)
    for copy in halos:
        copy.start()
    if beyond:
        for far in (lax.rem(ix + reach, count_x), lax.rem(ix + count_x - reach, count_x)):
            pl.semaphore_signal(relay_sem, inc=1, device_id=(iy, far), device_id_type=MESH)
    xc.start(1, reach)
    yc.start()

    halos[2].wait_recv()
    halos[3].wait_recv()
    p_south = strided(p_ref, 0)
    k_north = strided(ky_ref, ny - 1)
    from_south = south_in[1] * (south_in[0] - p_south)
    from_south = jnp.where(iy == 0, jnp.zeros_like(from_south), from_south)
    from_north = k_north * north_in[...]
    from_north = jnp.where(iy == count_y - 1, jnp.zeros_like(from_north), from_north)
    e_ref[pl.ds(0, nz, stride=ny), :] = strided(e_ref, 0) + from_south
    e_ref[pl.ds(ny - 1, nz, stride=ny), :] = strided(e_ref, ny - 1) + from_north
    halos[0].wait_recv()
    halos[1].wait_recv()
    from_west = west_in[1:2] * (west_in[0:1] - west_out[...])
    from_west = jnp.where(ix == 0, jnp.zeros_like(from_west), from_west)
    from_east = east_out[1:2] * east_in[...]
    from_east = jnp.where(ix == count_x - 1, jnp.zeros_like(from_east), from_east)
    line = lax.broadcasted_iota(jnp.int32, (nx, rows), 0)
    edges = jnp.where(line == 0, from_west, jnp.where(line == nx - 1, from_east, 0.0))
    explicit = e_ref[...] + jnp.transpose(edges)

    step_z = reduce_lines(
        explicit.reshape(planes), nz, major_low, major_high, z1_ref, z2_ref, zi_ref
    )

    right = step_z.reshape(rows, nx)
    turned = jnp.transpose(right)
    xv_ref[ix, 0:1] = jnp.sum(vt_ref[...] * turned, axis=0, keepdims=True)
    xv_ref[ix, 1:2] = jnp.sum(wt_ref[...] * turned, axis=0, keepdims=True)
    xv.start(1, reach)
    if beyond:
        pl.semaphore_wait(relay_sem, 2)
        xc.start(reach + 1)
        xv.start(reach + 1)

    yc.arrive()

    def y_block(j):
        return tuple(yc_ref[j, k] for k in range(4))

    whole = join_all([y_block(j) for j in range(members)], join)
    for k in range(4):
        yc2_ref[group, k] = whole[k]
    yc2.start()

    def saturated(d):
        return d * lax.rsqrt(1.0 + d * d)

    def relaxed(memory, d):
        target = saturated(d).reshape(1, nz, ny, nx)
        share = wi_ref[...].reshape(4, 1, ny, nx)
        return memory * iw_ref[...].reshape(4, 1, ny, nx) + share * target

    local_x = reduce_lines(right, nx, rolled_low, rolled_high, x1_ref, x2_ref, xi_ref)
    nm_ref[...] = relaxed(m_ref[...].reshape(4, nz, ny, nx), step_z).reshape(4 * rows, nx)
    e_ref[...] = local_x

    yc2.arrive()

    def y_group(j):
        return tuple(yc2_ref[j, k] for k in range(4))

    own_y = tuple(yc_ref[member, k] for k in range(4))
    zero, one = jnp.zeros_like(own_y[0]), jnp.ones_like(own_y[0])
    state, lows, _ = below([(j < group, y_group(j)) for j in range(groups - 1)], (zero, one, zero))
    _, low_members, low_states = below([(True, y_block(j)) for j in range(members)], state)
    uppers = list(range(groups - 1, 0, -1))
    state, highs, _ = above([(j > group, y_group(j)) for j in uppers], (zero, one))
    downward = list(range(members - 1, -1, -1))
    _, high_members, high_states = above([(True, y_block(j)) for j in downward], state)
    high_members, high_states = high_members[::-1], high_states[::-1]
    low_state, high_state = low_states[0], high_states[0]
    low_own, high_own = low_members[0], high_members[0]
    for j in range(1, members):
        low_state, high_state, low_own, high_own = jax.tree.map(
            lambda new, old: jnp.where(member == j, new, old),
            (low_states[j], high_states[j], low_members[j], high_members[j]),
            (low_state, high_state, low_own, high_own),
        )
    past_above, past_below = one, one
    for j in range(members):
        past_above = jnp.where(j > member, past_above * low_members[j][0], past_above)
        past_below = jnp.where(j < member, past_below * high_members[j][0], past_below)
    for n in range(members):
        ylow_ref[groups + n] = low_members[n][0]
        yhigh_ref[groups + n] = high_members[n][0]
    for n in range(groups - 1):
        ylow_ref[n] = lows[n][0]
        yhigh_ref[n] = highs[n][0]
    own_parts = own_factors(own_y, low_state, high_state)
    own_parts += (low_own[1], high_own[1], past_above, past_below)
    for n, part in enumerate(own_parts):
        yown_ref[n] = part

    xc.arrive()

    def x_block(j):
        return tuple(xc_ref[j, k : k + 1] for k in range(4))

    own_x = tuple(xc_ref[ix, k : k + 1] for k in range(4))
    zero, one = jnp.zeros_like(own_x[0]), jnp.ones_like(own_x[0])
    x_lower = [(j < ix, j) for j in range(count_x - 1)]
    x_upper = [(j > ix, j) for j in range(count_x - 1, 0, -1)]
    low_state, lows = below_fractions([(c, x_block(j)) for c, j in x_lower], (zero, one, zero))
    high_state, highs = above_fractions([(c, x_block(j)) for c, j in x_upper], (zero, one))
    factors = own_factors(own_x, low_state, high_state)
    low_bottom, high_bottom = 1.0 / low_state[1], 1.0 / high_state[1]

    xv.arrive()
    e_low, f_high = zero, zero
    for (counts, j), (bottom, past, mixed) in zip(x_lower, lows):
        got = bottom * xv_ref[j, 1:2] - mixed * xv_ref[j, 0:1] + past * e_low
        e_low = jnp.where(counts, got, e_low)
    for (counts, j), (bottom, past, mixed) in zip(x_upper, highs):
        got = bottom * xv_ref[j, 0:1] + mixed * xv_ref[j, 1:2] + past * f_high
        f_high = jnp.where(counts, got, f_high)
    e_low, f_high = e_low * low_bottom, f_high * high_bottom
    mine = (xv_ref[ix, 0:1], xv_ref[ix, 1:2])
    lower_in, upper_in = inflow(own_x, factors, mine, e_low, f_high)
    step_x = e_ref[...] + jnp.transpose(vt_ref[...] * lower_in + wt_ref[...] * upper_in)

    e_ref[...] = step_x
    right = jnp.stack([strided(e_ref, y) for y in range(ny)])
    first = jnp.sum(vs_ref[...] * right, axis=0)
    last = jnp.sum(ws_ref[...] * right, axis=0)
    upward = last - yown_ref[8] * first
    downwards = first + yown_ref[9] * last
    ys_ref[0], ys_ref[1] = downwards, upward
    ys_ref[2], ys_ref[3] = downwards * yown_ref[11], upward * yown_ref[10]
    yv_ref[iy] = jnp.zeros_like(first)

    def toward(to):
        outside = jnp.where(to // members == group, 0, 2)
        return ys_ref.at[outside + jnp.where(to > iy, 1, 0)]

    yv = Ring(yv_ref, (yv_send, yv_receive), along_y, at_y, toward)
    yv.start()

    yi_ref[...] = reduce_lines(right, ny, major_low, major_high, y1_ref, y2_ref, yi_ref)
    memory = m_ref[...].reshape(4, rows, nx)
    partly = relaxed(nm_ref[...].reshape(4, nz, ny, nx), e_ref[...])
    partly = (partly * iw_ref[...].reshape(4, 1, ny, nx)).reshape(4, rows, nx)
    nm_ref[...] = partly.reshape(4 * rows, nx)
    moved = partly - memory
    nf_ref[...] = f_ref[...] - (moved[0] + moved[1] + moved[2] + moved[3])
    stores = [
        pltpu.make_async_copy(nm_ref, memory_out, store_sem.at[0]),
        pltpu.make_async_copy(nf_ref, flux_out, store_sem.at[1]),
    ]
    for store in stores:
        store.start()

    yv.arrive()
    e_low, f_high = jnp.zeros_like(first), jnp.zeros_like(first)
    sums = []
    for j in range(groups):
        parts = [yv_ref[j * members + k] for k in range(members)]
        sums.append(join_all(parts, lambda a, b: a + b))
    for j in range(groups - 1):
        e_low = jnp.where(j < group, sums[j] + ylow_ref[j] * e_low, e_low)
    for n, j in enumerate(uppers):
        f_high = jnp.where(j > group, sums[j] + yhigh_ref[n] * f_high, f_high)
    for j in range(members - 1):
        got = yv_ref[group * members + j] + ylow_ref[groups + j] * e_low
        e_low = jnp.where(j < member, got, e_low)
    for j in downward[:-1]:
        got = yv_ref[group * members + j] + yhigh_ref[groups + j] * f_high
        f_high = jnp.where(j > member, got, f_high)
    own_y = tuple(yc_ref[member, k] for k in range(4))
    factors = tuple(yown_ref[n] for n in range(8))
    lower_in, upper_in = inflow(own_y, factors, (first, last), e_low, f_high)
    step_y = yi_ref[...] + vs_ref[...] * lower_in + ws_ref[...] * upper_in
    for y in range(ny):
        e_ref[pl.ds(y, nz, stride=ny), :] = step_y[y]
    final = pltpu.make_async_copy(e_ref, step_out, store_sem.at[2])
    final.start()
    for copy in halos:
        copy.wait_send()
    for ring in (xc, yc, xv, yc2, yv):
        ring.finish()
    for store in stores:
        store.wait()
    final.wait()


def last_relaxation(
    sizes, step_in, flux_in, memory_in, pressure_in, relax_in,
    pressure_out, flux_out, memory_out,
    s_ref, f_ref, m_ref, p_ref, r_ref, load_sem, store_sem,
):
    nz, ny, nx = sizes
    rows = nz * ny
    pairs = [
        (step_in, s_ref), (pressure_in, p_ref), (relax_in, r_ref),
        (memory_in, m_ref), (flux_in, f_ref),
    ]
    loads = [pltpu.make_async_copy(a, b, load_sem.at[k]) for k, (a, b) in enumerate(pairs)]
    for load in loads:
        load.start()
    pairs = [(p_ref, pressure_out), (m_ref, memory_out), (f_ref, flux_out)]
    stores = [pltpu.make_async_copy(a, b, store_sem.at[k]) for k, (a, b) in enumerate(pairs)]
    loads[0].wait()
    loads[1].wait()
    step = s_ref[...]
    p_ref[...] = p_ref[...] + step
    stores[0].start()
    loads[2].wait()
    target = (step * lax.rsqrt(1.0 + step * step)).reshape(nz, ny, nx)
    weight = r_ref[...].reshape(4, 1, ny, nx)
    share = weight / (1.0 + weight)
    loads[3].wait()
    memory = m_ref[...].reshape(4, nz, ny, nx) + share * target[None]
    m_ref[...] = memory.reshape(4 * rows, nx)
    stores[1].start()
    loads[4].wait()
    shares = (share[0] + share[1]) + (share[2] + share[3])
    f_ref[...] = f_ref[...] - (shares * target).reshape(rows, nx)
    stores[2].start()
    for store in stores:
        store.wait()


def local(mesh, pressure, fluid_flux, memory, lateral_faces, vertical_faces, relax_rates):
    nz, ny, nx = pressure.shape
    rows = nz * ny
    count_y, count_x = mesh.shape["gy"], mesh.shape["gx"]
    groups = 4 if count_y >= 16 else max(1, count_y // 2)
    members = count_y // groups
    sizes = (nz, ny, nx, count_x, members, groups)
    f32 = jnp.float32

    def vmem(*shape):
        return pltpu.VMEM(shape, f32)

    def dma(n):
        return pltpu.SemaphoreType.DMA((max(n, 1),))

    plane = (rows, nx)
    levels_x, levels_y, levels_z = (n.bit_length() - 1 for n in (nx, ny, nz))
    tile = (nz, nx)
    scratch = [
        vmem(*plane), vmem(*plane), vmem(4 * rows, nx), vmem(*plane), vmem(*plane),
        vmem(*plane), vmem(4 * ny, nx),
        vmem(*plane), vmem(4 * rows, nx),
        vmem(levels_x, *plane), vmem(levels_x, *plane), vmem(*plane),
        vmem(nx, rows), vmem(nx, rows),
        vmem(levels_y, ny, *tile), vmem(levels_y, ny, *tile), vmem(ny, *tile),
        vmem(ny, *tile), vmem(ny, *tile),
        vmem(levels_z, nz, ny, nx), vmem(levels_z, nz, ny, nx), vmem(nz, ny, nx),
        vmem(*plane), vmem(4 * ny, nx), vmem(4 * ny, nx),
        vmem(2, rows), vmem(1, rows), vmem(1, rows), vmem(2, rows),
        vmem(2, *tile), vmem(*tile), vmem(*tile), vmem(2, *tile),
        vmem(count_x, 4, rows), vmem(count_x, 2, rows),
        vmem(members, 4, *tile), vmem(groups, 4, *tile), vmem(count_y, *tile), vmem(4, *tile),
        vmem(members + groups, *tile), vmem(members + groups, *tile), vmem(12, *tile),
        dma(7), dma(3), dma(4), dma(4), pltpu.SemaphoreType.REGULAR,
    ]
    scratch += [pltpu.SemaphoreType.DMA] * 10
    anywhere = pl.BlockSpec(memory_space=pl.ANY)
    outs = pl.pallas_call(
        partial(kernel, sizes),
        out_shape=(
            jax.ShapeDtypeStruct(plane, f32),
            jax.ShapeDtypeStruct(plane, f32),
            jax.ShapeDtypeStruct((4 * rows, nx), f32),
        ),
        in_specs=[anywhere] * 6,
        out_specs=(anywhere,) * 3,
        scratch_shapes=scratch,
        compiler_params=pltpu.CompilerParams(
            collective_id=0, has_side_effects=True, vmem_limit_bytes=60 << 20
        ),
        name="adi_step",
    )(
        pressure.reshape(plane),
        fluid_flux.reshape(plane),
        memory.reshape(4 * rows, nx),
        lateral_faces.reshape(2 * rows, nx),
        vertical_faces.reshape(plane),
        relax_rates.reshape(4 * ny, nx),
    )
    step, flux, memory = outs
    next_pressure, next_flux, next_memory = pl.pallas_call(
        partial(last_relaxation, (nz, ny, nx)),
        out_shape=(
            jax.ShapeDtypeStruct(plane, f32),
            jax.ShapeDtypeStruct(plane, f32),
            jax.ShapeDtypeStruct((4 * rows, nx), f32),
        ),
        in_specs=[anywhere] * 5,
        out_specs=(anywhere,) * 3,
        scratch_shapes=[
            vmem(*plane), vmem(*plane), vmem(4 * rows, nx), vmem(*plane), vmem(4 * ny, nx),
            dma(5), dma(3),
        ],
        compiler_params=pltpu.CompilerParams(vmem_limit_bytes=60 << 20),
        name="last_relaxation",
    )(step, flux, memory, pressure.reshape(plane), relax_rates.reshape(4 * ny, nx))
    return (
        next_pressure.reshape(nz, ny, nx),
        next_flux.reshape(nz, ny, nx),
        next_memory.reshape(4, nz, ny, nx),
    )


def solution(mesh):
    in_specs = (
        P(None, "gy", "gx"),
        P(None, "gy", "gx"),
        P(None, None, "gy", "gx"),
        P(None, None, "gy", "gx"),
        P(None, "gy", "gx"),
        P(None, "gy", "gx"),
    )
    out_specs = (P(None, "gy", "gx"), P(None, "gy", "gx"), P(None, None, "gy", "gx"))
    return jax.shard_map(
        partial(local, mesh), mesh=mesh, in_specs=in_specs, out_specs=out_specs, check_vma=False
    )
```

```python
from functools import partial

import jax
import jax.numpy as jnp
from jax import lax
from jax.experimental import pallas as pl
from jax.experimental.pallas import tpu as pltpu
from jax.sharding import PartitionSpec as P

MESH = pl.DeviceIdType.MESH


def rolled_low(a, s):
    return pltpu.roll(a, s, axis=1)


def rolled_high(a, s):
    return pltpu.roll(a, a.shape[1] - s, axis=1)


def major_low(a, s):
    return jnp.concatenate([a[a.shape[0] - s :], a[: a.shape[0] - s]], axis=0)


def major_high(a, s):
    return jnp.concatenate([a[s:], a[:s]], axis=0)


def factor(half, position, n, low, high, k1_ref, k2_ref, inv_ref, ends):
    first, last = position == 0, position == n - 1
    zero = jnp.zeros_like(half)
    link = jnp.where(last, zero, half)
    main = 1.0 + half + jnp.where(first, zero, low(half, 1))
    columns = []
    if ends:
        one = jnp.ones_like(half)
        columns = [jnp.where(first, one, zero), jnp.where(last, one, zero)]
    s, level = 1, 0
    while s < n:
        inverse = 1.0 / main
        k2 = link * high(inverse, s)
        scaled = link * inverse
        k1 = low(scaled, s)
        k1_ref[level] = k1
        k2_ref[level] = k2
        columns = [v + k1 * low(v, s) + k2 * high(v, s) for v in columns]
        main = main - low(link * scaled, s) - link * k2
        link = k2 * high(link, s)
        s, level = 2 * s, level + 1
    inverse = 1.0 / main
    inv_ref[...] = inverse
    return [v * inverse for v in columns]


def reduce_lines(right, n, low, high, k1_ref, k2_ref, inv_ref):
    s, level = 1, 0
    while s < n:
        right = right + k1_ref[level] * low(right, s) + k2_ref[level] * high(right, s)
        s, level = 2 * s, level + 1
    return right * inv_ref[...]


def join(one, two):
    g1, c1, w1, h1 = one
    g2, c2, w2, h2 = two
    e1 = 1.0 - w1 * h1
    gh = g2 * h1
    d = 1.0 / (1.0 + gh * e1)
    up, down = c1 * h1 * d, c2 * h1 * d
    return g1 + up * gh * c1, up * c2, w2 - down * e1 * c2, h2


def join_all(blocks, combine):
    while len(blocks) > 1:
        blocks = [combine(blocks[k], blocks[k + 1]) for k in range(0, len(blocks), 2)]
    return blocks[0]


def below(blocks, state):
    top, bottom, h = state
    factors, states = [], []
    for counts, (gj, cj, wj, hj) in blocks:
        states.append((top, bottom, h))
        a = h * (bottom - top * h)
        new_bottom = bottom + gj * a
        new_top = wj * new_bottom - cj * cj * a
        t = cj / new_bottom
        factors.append((t * h * bottom, t * a))
        top = jnp.where(counts, new_top, top)
        bottom = jnp.where(counts, new_bottom, bottom)
        h = jnp.where(counts, hj, h)
    return (top, bottom, h), factors, states


def above(blocks, state):
    top, bottom = state
    factors, states = [], []
    for counts, (gj, cj, wj, hj) in blocks:
        states.append((top, bottom))
        ch = cj * hj
        new_bottom = bottom + top * (hj * (1.0 - wj * hj))
        new_top = gj * new_bottom + ch * ch * top
        t = ch / new_bottom
        factors.append((t * bottom, t * top * hj))
        top = jnp.where(counts, new_top, top)
        bottom = jnp.where(counts, new_bottom, bottom)
    return (top, bottom), factors, states


def below_fractions(blocks, state):
    top, bottom, h = state
    factors = []
    for counts, (gj, cj, wj, hj) in blocks:
        a = h * (bottom - top * h)
        new_bottom = bottom + gj * a
        mixed = cj * a
        factors.append((new_bottom, cj * h, mixed))
        new_top = wj * new_bottom - cj * mixed
        top = jnp.where(counts, new_top, top)
        bottom = jnp.where(counts, new_bottom, bottom)
        h = jnp.where(counts, hj, h)
    return (top, bottom, h), factors


def above_fractions(blocks, state):
    top, bottom = state
    factors = []
    for counts, (gj, cj, wj, hj) in blocks:
        ch = cj * hj
        new_bottom = bottom + top * (hj * (1.0 - wj * hj))
        factors.append((new_bottom, ch, ch * hj * top))
        new_top = gj * new_bottom + ch * ch * top
        top = jnp.where(counts, new_top, top)
        bottom = jnp.where(counts, new_bottom, bottom)
    return (top, bottom), factors


def own_factors(own, low_state, high_state):
    g, c, w, h = own
    top, bottom, h_low = low_state
    a = h_low * (bottom - top * h_low) / bottom
    gh = high_state[0] * h / high_state[1]
    p = h / (1.0 + gh)
    q = gh * p
    r1, r2, ca, cq = 1.0 + g * a, 1.0 - w * q, c * a, c * q
    inverse = 1.0 / (r1 * r2 + ca * cq)
    return (h_low, a, p, q, r1 * inverse, r2 * inverse, ca * inverse, cq * inverse)


def inflow(own, factors, mine, e_low, f_high):
    g, c, w, _ = own
    h_low, a, p, q, r1, r2, ca, cq = factors
    u, v = h_low * e_low, p * f_high
    s1 = mine[0] + g * u + c * v
    s2 = mine[1] + c * u + w * v
    return u - a * (r2 * s1 + cq * s2), v + q * (r1 * s2 - ca * s1)


class Steps:
    def __init__(self, sizes, index):
        self.sizes, self.index = sizes, index
        self.count = 1
        for size in sizes:
            self.count *= size

    def split(self, number):
        digits = []
        for size in self.sizes[::-1]:
            digits.append(number % size)
            number = number // size
        return digits[::-1]

    def to(self, k):
        place = 0
        for size, at, step in zip(self.sizes, self.split(self.index), self.split(k)):
            place = place * size + (lax.rem(at + step, size) if step else at)
        return place

    def hops(self, k):
        return sum(min(step, size - step) for size, step in zip(self.sizes, self.split(k)))

    def far_first(self, least=1, most=99):
        steps = [k for k in range(1, self.count) if least <= self.hops(k) <= most]
        return sorted(steps, key=lambda k: -self.hops(k))


class Ring:
    def __init__(self, buffer, sems, steps, device, source=None):
        self.buffer, self.steps, self.device = buffer, steps, device
        self.send, self.receive = sems
        self.source = source or (lambda to: buffer.at[steps.index])

    def start(self, least=1, most=99):
        for k in self.steps.far_first(least, most):
            to = self.steps.to(k)
            pltpu.make_async_remote_copy(
                src_ref=self.source(to),
                dst_ref=self.buffer.at[self.steps.index],
                send_sem=self.send,
                recv_sem=self.receive,
                device_id=self.device(to),
                device_id_type=MESH,
            ).start()

    def all(self):
        every = self.buffer.at[pl.ds(0, self.steps.count - 1)]
        return pltpu.make_async_remote_copy(
            src_ref=every,
            dst_ref=every,
            send_sem=self.send,
            recv_sem=self.receive,
            device_id=self.device(self.steps.to(1)),
            device_id_type=MESH,
        )

    def arrive(self):
        self.all().wait_recv()

    def finish(self):
        self.all().wait_send()


def kernel(
    sizes,
    pressure_in, flux_in, memory_in, lateral_in, vertical_in, relax_in,
    step_out, flux_out, memory_out,
    p_ref, f_ref, m_ref, kx_ref, ky_ref, kz_ref, relax_ref,
    nf_ref, nm_ref,
    x1_ref, x2_ref, xi_ref, vt_ref, wt_ref,
    y1_ref, y2_ref, yi_ref, vs_ref, ws_ref,
    z1_ref, z2_ref, zi_ref,
    e_ref, iw_ref, wi_ref,
    east_out, west_out, east_in, west_in,
    north_out, south_out, north_in, south_in,
    xc_ref, xv_ref, yc_ref, yc2_ref, yv_ref, ys_ref,
    ylow_ref, yhigh_ref, yown_ref,
    load_sem, store_sem, halo_send, halo_receive, relay_sem,
    xc_send, xc_receive, xv_send, xv_receive,
    yc_send, yc_receive, yc2_send, yc2_receive, yv_send, yv_receive,
):
    nz, ny, nx, count_x, members, groups = sizes
    rows = nz * ny
    count_y = members * groups
    iy, ix = lax.axis_index("gy"), lax.axis_index("gx")
    group, member = iy // members, lax.rem(iy, members)
    reach = max(1, count_x // 4)
    beyond = count_x // 2 > reach
    along_x = Steps((count_x,), ix)
    along_y = Steps((4, 4, 2) if count_y == 32 else (count_y,), iy)
    inside = Steps((members // 2, 2), member)
    between = Steps((groups,), group)

    def at_x(k):
        return (iy, k)

    def at_y(k):
        return (k, ix)

    def in_group(k):
        return (group * members + k, ix)

    def across(k):
        return (k * members + member, ix)

    loads = [
        pltpu.make_async_copy(source, target, load_sem.at[k])
        for k, (source, target) in enumerate(
            [
                (pressure_in, p_ref),
                (lateral_in.at[pl.ds(0, rows)], kx_ref),
                (lateral_in.at[pl.ds(rows, rows)], ky_ref),
                (vertical_in, kz_ref),
                (flux_in, f_ref),
                (memory_in, m_ref),
                (relax_in, relax_ref),
            ]
        )
    ]
    for load in loads:
        load.start()

    barrier = pltpu.get_barrier_semaphore()

    greeted = 0
    for steps, device, most in ((along_x, at_x, reach), (along_y, at_y, 99)):
        for k in steps.far_first(1, most):
            pl.semaphore_signal(
                barrier, inc=1, device_id=device(steps.to(k)), device_id_type=MESH
            )
            greeted += 1

    lanes = lax.broadcasted_iota(jnp.int32, (rows, nx), 1)
    zero_plane = jnp.zeros((rows, nx), jnp.float32)
    planes = (nz, ny, nx)

    def strided(ref, y):
        return ref[pl.ds(y, nz, stride=ny), :]

    for k in range(3):
        loads[k].wait()
    p = p_ref[...]
    kx = kx_ref[...]
    turned = jnp.transpose(jnp.where(lanes == 1, rolled_low(kx, 2), p))
    p_first, kx_last, p_last = turned[0:1], turned[1:2], turned[nx - 1 : nx]
    east_out[0:1] = p_last
    east_out[1:2] = kx_last
    west_out[...] = p_first
    north_out[0] = strided(p_ref, ny - 1)
    north_out[1] = strided(ky_ref, ny - 1)
    south_out[...] = strided(p_ref, 0)

    v, w = factor(0.5 * kx, lanes, nx, rolled_low, rolled_high, x1_ref, x2_ref, xi_ref, True)
    vt, wt = jnp.transpose(v), jnp.transpose(w)
    vt_ref[...] = vt
    wt_ref[...] = wt
    xc_ref[ix, 0:1] = vt[0:1]
    xc_ref[ix, 1:2] = vt[nx - 1 : nx]
    xc_ref[ix, 2:3] = wt[nx - 1 : nx]
    xc_ref[ix, 3:4] = 0.5 * kx_last

    half_y = 0.5 * jnp.stack([strided(ky_ref, y) for y in range(ny)])
    row = lax.broadcasted_iota(jnp.int32, half_y.shape, 0)
    vs, ws = factor(half_y, row, ny, major_low, major_high, y1_ref, y2_ref, yi_ref, True)
    vs_ref[...] = vs
    ws_ref[...] = ws
    yc_ref[member, 0] = vs[0]
    yc_ref[member, 1] = vs[ny - 1]
    yc_ref[member, 2] = ws[ny - 1]
    yc_ref[member, 3] = half_y[ny - 1]

    for k in range(3, 7):
        loads[k].wait()
    kz = kz_ref[...]
    half_z = 0.5 * kz.reshape(planes)
    plane = lax.broadcasted_iota(jnp.int32, planes, 0)
    factor(half_z, plane, nz, major_low, major_high, z1_ref, z2_ref, zi_ref, False)
    p = p_ref[...]
    kx = kx_ref[...]
    explicit = kx * (jnp.where(lanes == nx - 1, zero_plane, rolled_high(p, 1)) - p)
    explicit -= jnp.where(
        lanes == 0, zero_plane, rolled_low(kx, 1) * (p - rolled_low(p, 1))
    )
    gap = jnp.zeros((ny, nx), jnp.float32)
    flow = kz * (jnp.concatenate([p[ny:], gap], axis=0) - p)
    explicit += flow - jnp.concatenate([gap, flow[: rows - ny]], axis=0)
    memory = m_ref[...].reshape(4, rows, nx)
    e_ref[...] = explicit + (f_ref[...] - (memory[0] + memory[1] + memory[2] + memory[3]))
    previous = None
    for y in range(ny):
        k_here, p_here = strided(ky_ref, y), strided(p_ref, y)
        p_next = strided(p_ref, y + 1) if y + 1 < ny else jnp.zeros_like(p_here)
        flow = k_here * (p_next - p_here)
        along = flow if previous is None else flow - previous
        e_ref[pl.ds(y, nz, stride=ny), :] = strided(e_ref, y) + along
        previous = flow
    weight = relax_ref[...]
    inverse = 1.0 / (1.0 + weight)
    iw_ref[...] = inverse
    wi_ref[...] = weight * inverse

    north, south = lax.rem(iy + 1, count_y), lax.rem(iy + count_y - 1, count_y)
    east, west = lax.rem(ix + 1, count_x), lax.rem(ix + count_x - 1, count_x)

    def halo(k, source, target, device):
        return pltpu.make_async_remote_copy(
            src_ref=source,
            dst_ref=target,
            send_sem=halo_send.at[k],
            recv_sem=halo_receive.at[k],
            device_id=device,
            device_id_type=MESH,
        )

    halos = [
        halo(0, east_out, west_in, (iy, east)),
        halo(1, west_out, east_in, (iy, west)),
        halo(2, north_out, south_in, (north, ix)),
        halo(3, south_out, north_in, (south, ix)),
    ]
    xc = Ring(xc_ref, (xc_send, xc_receive), along_x, at_x)
    xv = Ring(xv_ref, (xv_send, xv_receive), along_x, at_x)
    yc = Ring(yc_ref, (yc_send, yc_receive), inside, in_group)
    yc2 = Ring(yc2_ref, (yc2_send, yc2_receive), between, across)

    pl.semaphore_wait(barrier, greeted)
    for copy in halos:
        copy.start()
    if beyond:
        for far in (lax.rem(ix + reach, count_x), lax.rem(ix + count_x - reach, count_x)):
            pl.semaphore_signal(relay_sem, inc=1, device_id=(iy, far), device_id_type=MESH)
    xc.start(1, reach)
    yc.start()

    halos[2].wait_recv()
    halos[3].wait_recv()
    p_south = strided(p_ref, 0)
    k_north = strided(ky_ref, ny - 1)
    from_south = south_in[1] * (south_in[0] - p_south)
    from_south = jnp.where(iy == 0, jnp.zeros_like(from_south), from_south)
    from_north = k_north * north_in[...]
    from_north = jnp.where(iy == count_y - 1, jnp.zeros_like(from_north), from_north)
    e_ref[pl.ds(0, nz, stride=ny), :] = strided(e_ref, 0) + from_south
    e_ref[pl.ds(ny - 1, nz, stride=ny), :] = strided(e_ref, ny - 1) + from_north
    halos[0].wait_recv()
    halos[1].wait_recv()
    from_west = west_in[1:2] * (west_in[0:1] - west_out[...])
    from_west = jnp.where(ix == 0, jnp.zeros_like(from_west), from_west)
    from_east = east_out[1:2] * east_in[...]
    from_east = jnp.where(ix == count_x - 1, jnp.zeros_like(from_east), from_east)
    line = lax.broadcasted_iota(jnp.int32, (nx, rows), 0)
    edges = jnp.where(line == 0, from_west, jnp.where(line == nx - 1, from_east, 0.0))
    explicit = e_ref[...] + jnp.transpose(edges)

    step_z = reduce_lines(
        explicit.reshape(planes), nz, major_low, major_high, z1_ref, z2_ref, zi_ref
    )

    right = step_z.reshape(rows, nx)
    turned = jnp.transpose(right)
    xv_ref[ix, 0:1] = jnp.sum(vt_ref[...] * turned, axis=0, keepdims=True)
    xv_ref[ix, 1:2] = jnp.sum(wt_ref[...] * turned, axis=0, keepdims=True)
    xv.start(1, reach)
    if beyond:
        pl.semaphore_wait(relay_sem, 2)
        xc.start(reach + 1)
        xv.start(reach + 1)

    yc.arrive()

    def y_block(j):
        return tuple(yc_ref[j, k] for k in range(4))

    whole = join_all([y_block(j) for j in range(members)], join)
    for k in range(4):
        yc2_ref[group, k] = whole[k]
    yc2.start()

    def saturated(d):
        return d * lax.rsqrt(1.0 + d * d)

    def relaxed(memory, d):
        target = saturated(d).reshape(1, nz, ny, nx)
        share = wi_ref[...].reshape(4, 1, ny, nx)
        return memory * iw_ref[...].reshape(4, 1, ny, nx) + share * target

    local_x = reduce_lines(right, nx, rolled_low, rolled_high, x1_ref, x2_ref, xi_ref)
    nm_ref[...] = relaxed(m_ref[...].reshape(4, nz, ny, nx), step_z).reshape(4 * rows, nx)
    e_ref[...] = local_x

    yc2.arrive()

    def y_group(j):
        return tuple(yc2_ref[j, k] for k in range(4))

    own_y = tuple(yc_ref[member, k] for k in range(4))
    zero, one = jnp.zeros_like(own_y[0]), jnp.ones_like(own_y[0])
    state, lows, _ = below([(j < group, y_group(j)) for j in range(groups - 1)], (zero, one, zero))
    _, low_members, low_states = below([(True, y_block(j)) for j in range(members)], state)
    uppers = list(range(groups - 1, 0, -1))
    state, highs, _ = above([(j > group, y_group(j)) for j in uppers], (zero, one))
    downward = list(range(members - 1, -1, -1))
    _, high_members, high_states = above([(True, y_block(j)) for j in downward], state)
    high_members, high_states = high_members[::-1], high_states[::-1]
    low_state, high_state = low_states[0], high_states[0]
    low_own, high_own = low_members[0], high_members[0]
    for j in range(1, members):
        low_state, high_state, low_own, high_own = jax.tree.map(
            lambda new, old: jnp.where(member == j, new, old),
            (low_states[j], high_states[j], low_members[j], high_members[j]),
            (low_state, high_state, low_own, high_own),
        )
    past_above, past_below = one, one
    for j in range(members):
        past_above = jnp.where(j > member, past_above * low_members[j][0], past_above)
        past_below = jnp.where(j < member, past_below * high_members[j][0], past_below)
    for n in range(members):
        ylow_ref[groups + n] = low_members[n][0]
        yhigh_ref[groups + n] = high_members[n][0]
    for n in range(groups - 1):
        ylow_ref[n] = lows[n][0]
        yhigh_ref[n] = highs[n][0]
    own_parts = own_factors(own_y, low_state, high_state)
    own_parts += (low_own[1], high_own[1], past_above, past_below)
    for n, part in enumerate(own_parts):
        yown_ref[n] = part

    xc.arrive()

    def x_block(j):
        return tuple(xc_ref[j, k : k + 1] for k in range(4))

    own_x = tuple(xc_ref[ix, k : k + 1] for k in range(4))
    zero, one = jnp.zeros_like(own_x[0]), jnp.ones_like(own_x[0])
    x_lower = [(j < ix, j) for j in range(count_x - 1)]
    x_upper = [(j > ix, j) for j in range(count_x - 1, 0, -1)]
    low_state, lows = below_fractions([(c, x_block(j)) for c, j in x_lower], (zero, one, zero))
    high_state, highs = above_fractions([(c, x_block(j)) for c, j in x_upper], (zero, one))
    factors = own_factors(own_x, low_state, high_state)
    low_bottom, high_bottom = 1.0 / low_state[1], 1.0 / high_state[1]

    xv.arrive()
    e_low, f_high = zero, zero
    for (counts, j), (bottom, past, mixed) in zip(x_lower, lows):
        got = bottom * xv_ref[j, 1:2] - mixed * xv_ref[j, 0:1] + past * e_low
        e_low = jnp.where(counts, got, e_low)
    for (counts, j), (bottom, past, mixed) in zip(x_upper, highs):
        got = bottom * xv_ref[j, 0:1] + mixed * xv_ref[j, 1:2] + past * f_high
        f_high = jnp.where(counts, got, f_high)
    e_low, f_high = e_low * low_bottom, f_high * high_bottom
    mine = (xv_ref[ix, 0:1], xv_ref[ix, 1:2])
    lower_in, upper_in = inflow(own_x, factors, mine, e_low, f_high)
    step_x = e_ref[...] + jnp.transpose(vt_ref[...] * lower_in + wt_ref[...] * upper_in)

    e_ref[...] = step_x
    right = jnp.stack([strided(e_ref, y) for y in range(ny)])
    first = jnp.sum(vs_ref[...] * right, axis=0)
    last = jnp.sum(ws_ref[...] * right, axis=0)
    upward = last - yown_ref[8] * first
    downwards = first + yown_ref[9] * last
    ys_ref[0], ys_ref[1] = downwards, upward
    ys_ref[2], ys_ref[3] = downwards * yown_ref[11], upward * yown_ref[10]
    yv_ref[iy] = jnp.zeros_like(first)

    def toward(to):
        outside = jnp.where(to // members == group, 0, 2)
        return ys_ref.at[outside + jnp.where(to > iy, 1, 0)]

    yv = Ring(yv_ref, (yv_send, yv_receive), along_y, at_y, toward)
    yv.start()

    yi_ref[...] = reduce_lines(right, ny, major_low, major_high, y1_ref, y2_ref, yi_ref)
    memory = m_ref[...].reshape(4, rows, nx)
    partly = relaxed(nm_ref[...].reshape(4, nz, ny, nx), e_ref[...])
    partly = (partly * iw_ref[...].reshape(4, 1, ny, nx)).reshape(4, rows, nx)
    nm_ref[...] = partly.reshape(4 * rows, nx)
    moved = partly - memory
    nf_ref[...] = f_ref[...] - (moved[0] + moved[1] + moved[2] + moved[3])
    stores = [
        pltpu.make_async_copy(nm_ref, memory_out, store_sem.at[0]),
        pltpu.make_async_copy(nf_ref, flux_out, store_sem.at[1]),
    ]
    for store in stores:
        store.start()

    yv.arrive()
    e_low, f_high = jnp.zeros_like(first), jnp.zeros_like(first)
    sums = []
    for j in range(groups):
        parts = [yv_ref[j * members + k] for k in range(members)]
        sums.append(join_all(parts, lambda a, b: a + b))
    for j in range(groups - 1):
        e_low = jnp.where(j < group, sums[j] + ylow_ref[j] * e_low, e_low)
    for n, j in enumerate(uppers):
        f_high = jnp.where(j > group, sums[j] + yhigh_ref[n] * f_high, f_high)
    for j in range(members - 1):
        got = yv_ref[group * members + j] + ylow_ref[groups + j] * e_low
        e_low = jnp.where(j < member, got, e_low)
    for j in downward[:-1]:
        got = yv_ref[group * members + j] + yhigh_ref[groups + j] * f_high
        f_high = jnp.where(j > member, got, f_high)
    own_y = tuple(yc_ref[member, k] for k in range(4))
    factors = tuple(yown_ref[n] for n in range(8))
    lower_in, upper_in = inflow(own_y, factors, (first, last), e_low, f_high)
    step_y = yi_ref[...] + vs_ref[...] * lower_in + ws_ref[...] * upper_in
    for y in range(ny):
        step_out[pl.ds(y, nz, stride=ny), :] = step_y[y]
    for copy in halos:
        copy.wait_send()
    for ring in (xc, yc, xv, yc2, yv):
        ring.finish()
    for store in stores:
        store.wait()


def last_relaxation(
    sizes, step_ref, flux_ref, memory_ref, pressure_ref, relax_ref,
    pressure_out, flux_out, memory_out,
    p_ref, f_ref, m_ref, store_sem,
):
    nz, ny, nx = sizes
    rows = nz * ny
    pairs = [(p_ref, pressure_out), (m_ref, memory_out), (f_ref, flux_out)]
    stores = [pltpu.make_async_copy(a, b, store_sem.at[k]) for k, (a, b) in enumerate(pairs)]
    step = step_ref[...]
    target = (step * lax.rsqrt(1.0 + step * step)).reshape(nz, ny, nx)
    weight = relax_ref[...].reshape(4, 1, ny, nx)
    share = weight / (1.0 + weight)
    memory = memory_ref[...].reshape(4, nz, ny, nx) + share * target[None]
    m_ref[...] = memory.reshape(4 * rows, nx)
    stores[1].start()
    p_ref[...] = pressure_ref[...] + step
    stores[0].start()
    shares = (share[0] + share[1]) + (share[2] + share[3])
    f_ref[...] = flux_ref[...] - (shares * target).reshape(rows, nx)
    stores[2].start()
    for store in stores:
        store.wait()


def local(mesh, pressure, fluid_flux, memory, lateral_faces, vertical_faces, relax_rates):
    nz, ny, nx = pressure.shape
    rows = nz * ny
    count_y, count_x = mesh.shape["gy"], mesh.shape["gx"]
    groups = 4 if count_y >= 16 else max(1, count_y // 2)
    members = count_y // groups
    sizes = (nz, ny, nx, count_x, members, groups)
    f32 = jnp.float32

    def vmem(*shape):
        return pltpu.VMEM(shape, f32)

    def dma(n):
        return pltpu.SemaphoreType.DMA((max(n, 1),))

    plane = (rows, nx)
    levels_x, levels_y, levels_z = (n.bit_length() - 1 for n in (nx, ny, nz))
    tile = (nz, nx)
    scratch = [
        vmem(*plane), vmem(*plane), vmem(4 * rows, nx), vmem(*plane), vmem(*plane),
        vmem(*plane), vmem(4 * ny, nx),
        vmem(*plane), vmem(4 * rows, nx),
        vmem(levels_x, *plane), vmem(levels_x, *plane), vmem(*plane),
        vmem(nx, rows), vmem(nx, rows),
        vmem(levels_y, ny, *tile), vmem(levels_y, ny, *tile), vmem(ny, *tile),
        vmem(ny, *tile), vmem(ny, *tile),
        vmem(levels_z, nz, ny, nx), vmem(levels_z, nz, ny, nx), vmem(nz, ny, nx),
        vmem(*plane), vmem(4 * ny, nx), vmem(4 * ny, nx),
        vmem(2, rows), vmem(1, rows), vmem(1, rows), vmem(2, rows),
        vmem(2, *tile), vmem(*tile), vmem(*tile), vmem(2, *tile),
        vmem(count_x, 4, rows), vmem(count_x, 2, rows),
        vmem(members, 4, *tile), vmem(groups, 4, *tile), vmem(count_y, *tile), vmem(4, *tile),
        vmem(members + groups, *tile), vmem(members + groups, *tile), vmem(12, *tile),
        dma(7), dma(2), dma(4), dma(4), pltpu.SemaphoreType.REGULAR,
    ]
    scratch += [pltpu.SemaphoreType.DMA] * 10
    anywhere = pl.BlockSpec(memory_space=pl.ANY)
    outs = pl.pallas_call(
        partial(kernel, sizes),
        out_shape=(
            jax.ShapeDtypeStruct(plane, f32),
            jax.ShapeDtypeStruct(plane, f32),
            jax.ShapeDtypeStruct((4 * rows, nx), f32),
        ),
        in_specs=[anywhere] * 6,
        out_specs=(pl.BlockSpec(memory_space=pltpu.VMEM), anywhere, anywhere),
        scratch_shapes=scratch,
        compiler_params=pltpu.CompilerParams(
            collective_id=0, has_side_effects=True, vmem_limit_bytes=24 << 20
        ),
        name="adi_step",
    )(
        *(
            pltpu.with_memory_space_constraint(a, pltpu.HBM)
            for a in (
                pressure.reshape(plane),
                fluid_flux.reshape(plane),
                memory.reshape(4 * rows, nx),
                lateral_faces.reshape(2 * rows, nx),
                vertical_faces.reshape(plane),
                relax_rates.reshape(4 * ny, nx),
            )
        )
    )
    step, flux, memory = outs
    next_pressure, next_flux, next_memory = pl.pallas_call(
        partial(last_relaxation, (nz, ny, nx)),
        out_shape=(
            jax.ShapeDtypeStruct(plane, f32),
            jax.ShapeDtypeStruct(plane, f32),
            jax.ShapeDtypeStruct((4 * rows, nx), f32),
        ),
        in_specs=[pl.BlockSpec(memory_space=pltpu.VMEM)] * 5,
        out_specs=(anywhere,) * 3,
        scratch_shapes=[
            vmem(*plane), vmem(*plane), vmem(4 * rows, nx), dma(3),
        ],
        compiler_params=pltpu.CompilerParams(vmem_limit_bytes=24 << 20),
        name="last_relaxation",
    )(step, flux, memory, pressure.reshape(plane), relax_rates.reshape(4 * ny, nx))
    return (
        next_pressure.reshape(nz, ny, nx),
        next_flux.reshape(nz, ny, nx),
        next_memory.reshape(4, nz, ny, nx),
    )


def solution(mesh):
    in_specs = (
        P(None, "gy", "gx"),
        P(None, "gy", "gx"),
        P(None, None, "gy", "gx"),
        P(None, None, "gy", "gx"),
        P(None, "gy", "gx"),
        P(None, "gy", "gx"),
    )
    out_specs = (P(None, "gy", "gx"), P(None, "gy", "gx"), P(None, None, "gy", "gx"))
    return jax.shard_map(
        partial(local, mesh), mesh=mesh, in_specs=in_specs, out_specs=out_specs, check_vma=False
    )
```

```python
from functools import partial

import jax
import jax.numpy as jnp
from jax import lax
from jax.experimental import pallas as pl
from jax.experimental.pallas import tpu as pltpu
from jax.sharding import PartitionSpec as P

MESH = pl.DeviceIdType.MESH


def rolled_low(a, s):
    return pltpu.roll(a, s, axis=1)


def rolled_high(a, s):
    return pltpu.roll(a, a.shape[1] - s, axis=1)


def major_low(a, s):
    return jnp.concatenate([a[a.shape[0] - s :], a[: a.shape[0] - s]], axis=0)


def major_high(a, s):
    return jnp.concatenate([a[s:], a[:s]], axis=0)


def factor(half, position, n, low, high, k1_ref, k2_ref, inv_ref, ends):
    first, last = position == 0, position == n - 1
    zero = jnp.zeros_like(half)
    link = jnp.where(last, zero, half)
    main = 1.0 + half + jnp.where(first, zero, low(half, 1))
    columns = []
    if ends:
        one = jnp.ones_like(half)
        columns = [jnp.where(first, one, zero), jnp.where(last, one, zero)]
    s, level = 1, 0
    while s < n:
        inverse = 1.0 / main
        k2 = link * high(inverse, s)
        scaled = link * inverse
        k1 = low(scaled, s)
        k1_ref[level] = k1
        k2_ref[level] = k2
        columns = [v + k1 * low(v, s) + k2 * high(v, s) for v in columns]
        main = main - low(link * scaled, s) - link * k2
        link = k2 * high(link, s)
        s, level = 2 * s, level + 1
    inverse = 1.0 / main
    inv_ref[...] = inverse
    return [v * inverse for v in columns]


def reduce_lines(right, n, low, high, k1_ref, k2_ref, inv_ref):
    s, level = 1, 0
    while s < n:
        right = right + k1_ref[level] * low(right, s) + k2_ref[level] * high(right, s)
        s, level = 2 * s, level + 1
    return right * inv_ref[...]


def join(one, two):
    g1, c1, w1, h1 = one
    g2, c2, w2, h2 = two
    e1 = 1.0 - w1 * h1
    gh = g2 * h1
    d = 1.0 / (1.0 + gh * e1)
    up, down = c1 * h1 * d, c2 * h1 * d
    return g1 + up * gh * c1, up * c2, w2 - down * e1 * c2, h2


def join_all(blocks, combine):
    while len(blocks) > 1:
        blocks = [combine(blocks[k], blocks[k + 1]) for k in range(0, len(blocks), 2)]
    return blocks[0]


def below(blocks, state):
    top, bottom, h = state
    factors, states = [], []
    for counts, (gj, cj, wj, hj) in blocks:
        states.append((top, bottom, h))
        a = h * (bottom - top * h)
        new_bottom = bottom + gj * a
        new_top = wj * new_bottom - cj * cj * a
        t = cj / new_bottom
        factors.append((t * h * bottom, t * a))
        top = jnp.where(counts, new_top, top)
        bottom = jnp.where(counts, new_bottom, bottom)
        h = jnp.where(counts, hj, h)
    return (top, bottom, h), factors, states


def above(blocks, state):
    top, bottom = state
    factors, states = [], []
    for counts, (gj, cj, wj, hj) in blocks:
        states.append((top, bottom))
        ch = cj * hj
        new_bottom = bottom + top * (hj * (1.0 - wj * hj))
        new_top = gj * new_bottom + ch * ch * top
        t = ch / new_bottom
        factors.append((t * bottom, t * top * hj))
        top = jnp.where(counts, new_top, top)
        bottom = jnp.where(counts, new_bottom, bottom)
    return (top, bottom), factors, states


def below_fractions(blocks, state):
    top, bottom, h = state
    factors = []
    for counts, (gj, cj, wj, hj) in blocks:
        a = h * (bottom - top * h)
        new_bottom = bottom + gj * a
        mixed = cj * a
        factors.append((new_bottom, cj * h, mixed))
        new_top = wj * new_bottom - cj * mixed
        top = jnp.where(counts, new_top, top)
        bottom = jnp.where(counts, new_bottom, bottom)
        h = jnp.where(counts, hj, h)
    return (top, bottom, h), factors


def above_fractions(blocks, state):
    top, bottom = state
    factors = []
    for counts, (gj, cj, wj, hj) in blocks:
        ch = cj * hj
        new_bottom = bottom + top * (hj * (1.0 - wj * hj))
        factors.append((new_bottom, ch, ch * hj * top))
        new_top = gj * new_bottom + ch * ch * top
        top = jnp.where(counts, new_top, top)
        bottom = jnp.where(counts, new_bottom, bottom)
    return (top, bottom), factors


def own_factors(own, low_state, high_state):
    g, c, w, h = own
    top, bottom, h_low = low_state
    a = h_low * (bottom - top * h_low) / bottom
    gh = high_state[0] * h / high_state[1]
    p = h / (1.0 + gh)
    q = gh * p
    r1, r2, ca, cq = 1.0 + g * a, 1.0 - w * q, c * a, c * q
    inverse = 1.0 / (r1 * r2 + ca * cq)
    return (h_low, a, p, q, r1 * inverse, r2 * inverse, ca * inverse, cq * inverse)


def inflow(own, factors, mine, e_low, f_high):
    g, c, w, _ = own
    h_low, a, p, q, r1, r2, ca, cq = factors
    u, v = h_low * e_low, p * f_high
    s1 = mine[0] + g * u + c * v
    s2 = mine[1] + c * u + w * v
    return u - a * (r2 * s1 + cq * s2), v + q * (r1 * s2 - ca * s1)


class Steps:
    def __init__(self, sizes, index):
        self.sizes, self.index = sizes, index
        self.count = 1
        for size in sizes:
            self.count *= size

    def split(self, number):
        digits = []
        for size in self.sizes[::-1]:
            digits.append(number % size)
            number = number // size
        return digits[::-1]

    def to(self, k):
        place = 0
        for size, at, step in zip(self.sizes, self.split(self.index), self.split(k)):
            place = place * size + (lax.rem(at + step, size) if step else at)
        return place

    def hops(self, k):
        return sum(min(step, size - step) for size, step in zip(self.sizes, self.split(k)))

    def far_first(self, least=1, most=99):
        steps = [k for k in range(1, self.count) if least <= self.hops(k) <= most]
        return sorted(steps, key=lambda k: -self.hops(k))


class Ring:
    def __init__(self, buffer, sems, steps, device, source=None):
        self.buffer, self.steps, self.device = buffer, steps, device
        self.send, self.receive = sems
        self.source = source or (lambda to: buffer.at[steps.index])

    def start(self, least=1, most=99):
        for k in self.steps.far_first(least, most):
            to = self.steps.to(k)
            pltpu.make_async_remote_copy(
                src_ref=self.source(to),
                dst_ref=self.buffer.at[self.steps.index],
                send_sem=self.send,
                recv_sem=self.receive,
                device_id=self.device(to),
                device_id_type=MESH,
            ).start()

    def all(self):
        every = self.buffer.at[pl.ds(0, self.steps.count - 1)]
        return pltpu.make_async_remote_copy(
            src_ref=every,
            dst_ref=every,
            send_sem=self.send,
            recv_sem=self.receive,
            device_id=self.device(self.steps.to(1)),
            device_id_type=MESH,
        )

    def arrive(self):
        self.all().wait_recv()

    def finish(self):
        self.all().wait_send()


def kernel(
    sizes,
    pressure_in, flux_in, memory_in, lateral_in, vertical_in, relax_in,
    step_out, flux_out, memory_out,
    p_ref, f_ref, m_ref, kx_ref, ky_ref, kz_ref, relax_ref,
    nf_ref, nm_ref,
    x1_ref, x2_ref, xi_ref, vt_ref, wt_ref,
    y1_ref, y2_ref, yi_ref, vs_ref, ws_ref,
    z1_ref, z2_ref, zi_ref,
    e_ref, iw_ref, wi_ref,
    east_out, west_out, east_in, west_in,
    north_out, south_out, north_in, south_in,
    xc_ref, xv_ref, yc_ref, yc2_ref, yv_ref, ys_ref,
    ylow_ref, yhigh_ref, yown_ref,
    load_sem, store_sem, halo_send, halo_receive, relay_sem,
    xc_send, xc_receive, xv_send, xv_receive,
    yc_send, yc_receive, yc2_send, yc2_receive, yv_send, yv_receive,
):
    nz, ny, nx, count_x, members, groups = sizes
    rows = nz * ny
    count_y = members * groups
    iy, ix = lax.axis_index("gy"), lax.axis_index("gx")
    group, member = iy // members, lax.rem(iy, members)
    reach = max(1, count_x // 4)
    beyond = count_x // 2 > reach
    along_x = Steps((count_x,), ix)
    along_y = Steps((4, 4, 2) if count_y == 32 else (count_y,), iy)
    inside = Steps((members // 2, 2), member)
    between = Steps((groups,), group)

    def at_x(k):
        return (iy, k)

    def at_y(k):
        return (k, ix)

    def in_group(k):
        return (group * members + k, ix)

    def across(k):
        return (k * members + member, ix)

    loads = [
        pltpu.make_async_copy(source, target, load_sem.at[k])
        for k, (source, target) in enumerate(
            [
                (pressure_in, p_ref),
                (lateral_in.at[pl.ds(0, rows)], kx_ref),
                (lateral_in.at[pl.ds(rows, rows)], ky_ref),
                (vertical_in, kz_ref),
                (flux_in, f_ref),
                (memory_in, m_ref),
                (relax_in, relax_ref),
            ]
        )
    ]
    for load in loads:
        load.start()

    barrier = pltpu.get_barrier_semaphore()

    north, south = lax.rem(iy + 1, count_y), lax.rem(iy + count_y - 1, count_y)
    east, west = lax.rem(ix + 1, count_x), lax.rem(ix + count_x - 1, count_x)
    greeted = [
        device(steps.to(k))
        for steps, device, most in (
            (along_x, at_x, reach), (between, across, 99), (inside, in_group, 99)
        )
        for k in steps.far_first(1, most)
    ] + [at_y(north), at_y(south)]
    for device in greeted:
        pl.semaphore_signal(barrier, inc=1, device_id=device, device_id_type=MESH)

    lanes = lax.broadcasted_iota(jnp.int32, (rows, nx), 1)
    zero_plane = jnp.zeros((rows, nx), jnp.float32)
    planes = (nz, ny, nx)

    def strided(ref, y):
        return ref[pl.ds(y, nz, stride=ny), :]

    for k in range(3):
        loads[k].wait()
    p = p_ref[...]
    kx = kx_ref[...]
    turned = jnp.transpose(jnp.where(lanes == 1, rolled_low(kx, 2), p))
    p_first, kx_last, p_last = turned[0:1], turned[1:2], turned[nx - 1 : nx]
    east_out[0:1] = p_last
    east_out[1:2] = kx_last
    west_out[...] = p_first
    north_out[0] = strided(p_ref, ny - 1)
    north_out[1] = strided(ky_ref, ny - 1)
    south_out[...] = strided(p_ref, 0)

    v, w = factor(0.5 * kx, lanes, nx, rolled_low, rolled_high, x1_ref, x2_ref, xi_ref, True)
    vt, wt = jnp.transpose(v), jnp.transpose(w)
    vt_ref[...] = vt
    wt_ref[...] = wt
    xc_ref[ix, 0:1] = vt[0:1]
    xc_ref[ix, 1:2] = vt[nx - 1 : nx]
    xc_ref[ix, 2:3] = wt[nx - 1 : nx]
    xc_ref[ix, 3:4] = 0.5 * kx_last

    half_y = 0.5 * jnp.stack([strided(ky_ref, y) for y in range(ny)])
    row = lax.broadcasted_iota(jnp.int32, half_y.shape, 0)
    vs, ws = factor(half_y, row, ny, major_low, major_high, y1_ref, y2_ref, yi_ref, True)
    vs_ref[...] = vs
    ws_ref[...] = ws
    yc_ref[member, 0] = vs[0]
    yc_ref[member, 1] = vs[ny - 1]
    yc_ref[member, 2] = ws[ny - 1]
    yc_ref[member, 3] = half_y[ny - 1]

    for k in range(3, 7):
        loads[k].wait()
    kz = kz_ref[...]
    half_z = 0.5 * kz.reshape(planes)
    plane = lax.broadcasted_iota(jnp.int32, planes, 0)
    factor(half_z, plane, nz, major_low, major_high, z1_ref, z2_ref, zi_ref, False)
    p = p_ref[...]
    kx = kx_ref[...]
    explicit = kx * (jnp.where(lanes == nx - 1, zero_plane, rolled_high(p, 1)) - p)
    explicit -= jnp.where(
        lanes == 0, zero_plane, rolled_low(kx, 1) * (p - rolled_low(p, 1))
    )
    gap = jnp.zeros((ny, nx), jnp.float32)
    flow = kz * (jnp.concatenate([p[ny:], gap], axis=0) - p)
    explicit += flow - jnp.concatenate([gap, flow[: rows - ny]], axis=0)
    memory = m_ref[...].reshape(4, rows, nx)
    e_ref[...] = explicit + (f_ref[...] - (memory[0] + memory[1] + memory[2] + memory[3]))
    previous = None
    for y in range(ny):
        k_here, p_here = strided(ky_ref, y), strided(p_ref, y)
        p_next = strided(p_ref, y + 1) if y + 1 < ny else jnp.zeros_like(p_here)
        flow = k_here * (p_next - p_here)
        along = flow if previous is None else flow - previous
        e_ref[pl.ds(y, nz, stride=ny), :] = strided(e_ref, y) + along
        previous = flow
    weight = relax_ref[...]
    inverse = 1.0 / (1.0 + weight)
    iw_ref[...] = inverse
    wi_ref[...] = weight * inverse

    def halo(k, source, target, device):
        return pltpu.make_async_remote_copy(
            src_ref=source,
            dst_ref=target,
            send_sem=halo_send.at[k],
            recv_sem=halo_receive.at[k],
            device_id=device,
            device_id_type=MESH,
        )

    halos = [
        halo(0, east_out, west_in, (iy, east)),
        halo(1, west_out, east_in, (iy, west)),
        halo(2, north_out, south_in, (north, ix)),
        halo(3, south_out, north_in, (south, ix)),
    ]
    xc = Ring(xc_ref, (xc_send, xc_receive), along_x, at_x)
    xv = Ring(xv_ref, (xv_send, xv_receive), along_x, at_x)
    yc = Ring(yc_ref, (yc_send, yc_receive), inside, in_group)
    yc2 = Ring(yc2_ref, (yc2_send, yc2_receive), between, across)

    pl.semaphore_wait(barrier, len(greeted))
    if beyond:
        for far in (lax.rem(ix + reach, count_x), lax.rem(ix + count_x - reach, count_x)):
            pl.semaphore_signal(
                relay_sem.at[0], inc=1, device_id=(iy, far), device_id_type=MESH
            )
    for copy in halos:
        copy.start()
    for k in between.far_first():
        pl.semaphore_signal(
            relay_sem.at[1], inc=1, device_id=across(between.to(k)), device_id_type=MESH
        )
    xc.start(1, reach)
    yc.start()

    halos[2].wait_recv()
    halos[3].wait_recv()
    p_south = strided(p_ref, 0)
    k_north = strided(ky_ref, ny - 1)
    from_south = south_in[1] * (south_in[0] - p_south)
    from_south = jnp.where(iy == 0, jnp.zeros_like(from_south), from_south)
    from_north = k_north * north_in[...]
    from_north = jnp.where(iy == count_y - 1, jnp.zeros_like(from_north), from_north)
    e_ref[pl.ds(0, nz, stride=ny), :] = strided(e_ref, 0) + from_south
    e_ref[pl.ds(ny - 1, nz, stride=ny), :] = strided(e_ref, ny - 1) + from_north
    halos[0].wait_recv()
    halos[1].wait_recv()
    from_west = west_in[1:2] * (west_in[0:1] - west_out[...])
    from_west = jnp.where(ix == 0, jnp.zeros_like(from_west), from_west)
    from_east = east_out[1:2] * east_in[...]
    from_east = jnp.where(ix == count_x - 1, jnp.zeros_like(from_east), from_east)
    line = lax.broadcasted_iota(jnp.int32, (nx, rows), 0)
    edges = jnp.where(line == 0, from_west, jnp.where(line == nx - 1, from_east, 0.0))
    explicit = e_ref[...] + jnp.transpose(edges)

    step_z = reduce_lines(
        explicit.reshape(planes), nz, major_low, major_high, z1_ref, z2_ref, zi_ref
    )

    right = step_z.reshape(rows, nx)
    turned = jnp.transpose(right)
    xv_ref[ix, 0:1] = jnp.sum(vt_ref[...] * turned, axis=0, keepdims=True)
    xv_ref[ix, 1:2] = jnp.sum(wt_ref[...] * turned, axis=0, keepdims=True)
    xv.start(1, reach)
    if beyond:
        pl.semaphore_wait(relay_sem.at[0], 2)
        for hops in range(count_x // 2, reach, -1):
            xc.start(hops, hops)
            xv.start(hops, hops)

    yc.arrive()

    def y_block(j):
        return tuple(yc_ref[j, k] for k in range(4))

    whole = join_all([y_block(j) for j in range(members)], join)
    for k in range(4):
        yc2_ref[group, k] = whole[k]
    yc2.start()

    def saturated(d):
        return d * lax.rsqrt(1.0 + d * d)

    def relaxed(memory, d):
        target = saturated(d).reshape(1, nz, ny, nx)
        share = wi_ref[...].reshape(4, 1, ny, nx)
        return memory * iw_ref[...].reshape(4, 1, ny, nx) + share * target

    local_x = reduce_lines(right, nx, rolled_low, rolled_high, x1_ref, x2_ref, xi_ref)
    nm_ref[...] = relaxed(m_ref[...].reshape(4, nz, ny, nx), step_z).reshape(4 * rows, nx)
    e_ref[...] = local_x

    yc2.arrive()

    def y_group(j):
        return tuple(yc2_ref[j, k] for k in range(4))

    own_y = tuple(yc_ref[member, k] for k in range(4))
    zero, one = jnp.zeros_like(own_y[0]), jnp.ones_like(own_y[0])
    state, lows, _ = below([(j < group, y_group(j)) for j in range(groups - 1)], (zero, one, zero))
    _, low_members, low_states = below([(True, y_block(j)) for j in range(members)], state)
    uppers = list(range(groups - 1, 0, -1))
    state, highs, _ = above([(j > group, y_group(j)) for j in uppers], (zero, one))
    downward = list(range(members - 1, -1, -1))
    _, high_members, high_states = above([(True, y_block(j)) for j in downward], state)
    high_members, high_states = high_members[::-1], high_states[::-1]
    low_state, high_state = low_states[0], high_states[0]
    low_own, high_own = low_members[0], high_members[0]
    for j in range(1, members):
        low_state, high_state, low_own, high_own = jax.tree.map(
            lambda new, old: jnp.where(member == j, new, old),
            (low_states[j], high_states[j], low_members[j], high_members[j]),
            (low_state, high_state, low_own, high_own),
        )
    past_above, past_below = one, one
    for j in range(members):
        past_above = jnp.where(j > member, past_above * low_members[j][0], past_above)
        past_below = jnp.where(j < member, past_below * high_members[j][0], past_below)
    for n in range(members):
        ylow_ref[groups + n] = low_members[n][0]
        yhigh_ref[groups + n] = high_members[n][0]
    for n in range(groups - 1):
        ylow_ref[n] = lows[n][0]
        yhigh_ref[n] = highs[n][0]
    own_parts = own_factors(own_y, low_state, high_state)
    own_parts += (low_own[1], high_own[1], past_above, past_below)
    for n, part in enumerate(own_parts):
        yown_ref[n] = part

    xc.arrive()

    def x_block(j):
        return tuple(xc_ref[j, k : k + 1] for k in range(4))

    own_x = tuple(xc_ref[ix, k : k + 1] for k in range(4))
    zero, one = jnp.zeros_like(own_x[0]), jnp.ones_like(own_x[0])
    x_lower = [(j < ix, j) for j in range(count_x - 1)]
    x_upper = [(j > ix, j) for j in range(count_x - 1, 0, -1)]
    low_state, lows = below_fractions([(c, x_block(j)) for c, j in x_lower], (zero, one, zero))
    high_state, highs = above_fractions([(c, x_block(j)) for c, j in x_upper], (zero, one))
    factors = own_factors(own_x, low_state, high_state)
    low_bottom, high_bottom = 1.0 / low_state[1], 1.0 / high_state[1]

    xv.arrive()
    e_low, f_high = zero, zero
    for (counts, j), (bottom, past, mixed) in zip(x_lower, lows):
        got = bottom * xv_ref[j, 1:2] - mixed * xv_ref[j, 0:1] + past * e_low
        e_low = jnp.where(counts, got, e_low)
    for (counts, j), (bottom, past, mixed) in zip(x_upper, highs):
        got = bottom * xv_ref[j, 0:1] + mixed * xv_ref[j, 1:2] + past * f_high
        f_high = jnp.where(counts, got, f_high)
    e_low, f_high = e_low * low_bottom, f_high * high_bottom
    mine = (xv_ref[ix, 0:1], xv_ref[ix, 1:2])
    lower_in, upper_in = inflow(own_x, factors, mine, e_low, f_high)
    step_x = e_ref[...] + jnp.transpose(vt_ref[...] * lower_in + wt_ref[...] * upper_in)

    e_ref[...] = step_x
    right = jnp.stack([strided(e_ref, y) for y in range(ny)])
    first = jnp.sum(vs_ref[...] * right, axis=0)
    last = jnp.sum(ws_ref[...] * right, axis=0)
    upward = last - yown_ref[8] * first
    downwards = first + yown_ref[9] * last
    ys_ref[0], ys_ref[1] = downwards, upward
    ys_ref[2], ys_ref[3] = downwards * yown_ref[11], upward * yown_ref[10]
    yv_ref[iy] = jnp.zeros_like(first)

    def toward(to):
        outside = jnp.where(to // members == group, 0, 2)
        return ys_ref.at[outside + jnp.where(to > iy, 1, 0)]

    yv = Ring(yv_ref, (yv_send, yv_receive), along_y, at_y, toward)
    if groups > 1:
        pl.semaphore_wait(relay_sem.at[1], groups - 1)
    yv.start()

    yi_ref[...] = reduce_lines(right, ny, major_low, major_high, y1_ref, y2_ref, yi_ref)
    memory = m_ref[...].reshape(4, rows, nx)
    partly = relaxed(nm_ref[...].reshape(4, nz, ny, nx), e_ref[...])
    partly = (partly * iw_ref[...].reshape(4, 1, ny, nx)).reshape(4, rows, nx)
    nm_ref[...] = partly.reshape(4 * rows, nx)
    moved = partly - memory
    nf_ref[...] = f_ref[...] - (moved[0] + moved[1] + moved[2] + moved[3])
    stores = [
        pltpu.make_async_copy(nm_ref, memory_out, store_sem.at[0]),
        pltpu.make_async_copy(nf_ref, flux_out, store_sem.at[1]),
    ]
    for store in stores:
        store.start()

    yv.arrive()
    e_low, f_high = jnp.zeros_like(first), jnp.zeros_like(first)
    sums = []
    for j in range(groups):
        parts = [yv_ref[j * members + k] for k in range(members)]
        sums.append(join_all(parts, lambda a, b: a + b))
    for j in range(groups - 1):
        e_low = jnp.where(j < group, sums[j] + ylow_ref[j] * e_low, e_low)
    for n, j in enumerate(uppers):
        f_high = jnp.where(j > group, sums[j] + yhigh_ref[n] * f_high, f_high)
    for j in range(members - 1):
        got = yv_ref[group * members + j] + ylow_ref[groups + j] * e_low
        e_low = jnp.where(j < member, got, e_low)
    for j in downward[:-1]:
        got = yv_ref[group * members + j] + yhigh_ref[groups + j] * f_high
        f_high = jnp.where(j > member, got, f_high)
    own_y = tuple(yc_ref[member, k] for k in range(4))
    factors = tuple(yown_ref[n] for n in range(8))
    lower_in, upper_in = inflow(own_y, factors, (first, last), e_low, f_high)
    step_y = yi_ref[...] + vs_ref[...] * lower_in + ws_ref[...] * upper_in
    for y in range(ny):
        step_out[pl.ds(y, nz, stride=ny), :] = step_y[y]
    for copy in halos:
        copy.wait_send()
    for ring in (xc, yc, xv, yc2, yv):
        ring.finish()
    for store in stores:
        store.wait()


def last_relaxation(
    sizes, step_ref, flux_ref, memory_ref, pressure_ref, relax_ref,
    pressure_out, flux_out, memory_out,
    p_ref, f_ref, m_ref, store_sem,
):
    nz, ny, nx = sizes
    rows = nz * ny
    pairs = [(p_ref, pressure_out), (m_ref, memory_out), (f_ref, flux_out)]
    stores = [pltpu.make_async_copy(a, b, store_sem.at[k]) for k, (a, b) in enumerate(pairs)]
    step = step_ref[...]
    target = (step * lax.rsqrt(1.0 + step * step)).reshape(nz, ny, nx)
    weight = relax_ref[...].reshape(4, 1, ny, nx)
    share = weight / (1.0 + weight)
    memory = memory_ref[...].reshape(4, nz, ny, nx) + share * target[None]
    m_ref[...] = memory.reshape(4 * rows, nx)
    stores[1].start()
    p_ref[...] = pressure_ref[...] + step
    stores[0].start()
    shares = (share[0] + share[1]) + (share[2] + share[3])
    f_ref[...] = flux_ref[...] - (shares * target).reshape(rows, nx)
    stores[2].start()
    for store in stores:
        store.wait()


def local(mesh, pressure, fluid_flux, memory, lateral_faces, vertical_faces, relax_rates):
    nz, ny, nx = pressure.shape
    rows = nz * ny
    count_y, count_x = mesh.shape["gy"], mesh.shape["gx"]
    groups = 4 if count_y >= 16 else max(1, count_y // 2)
    members = count_y // groups
    sizes = (nz, ny, nx, count_x, members, groups)
    f32 = jnp.float32

    def vmem(*shape):
        return pltpu.VMEM(shape, f32)

    def dma(n):
        return pltpu.SemaphoreType.DMA((max(n, 1),))

    plane = (rows, nx)
    levels_x, levels_y, levels_z = (n.bit_length() - 1 for n in (nx, ny, nz))
    tile = (nz, nx)
    scratch = [
        vmem(*plane), vmem(*plane), vmem(4 * rows, nx), vmem(*plane), vmem(*plane),
        vmem(*plane), vmem(4 * ny, nx),
        vmem(*plane), vmem(4 * rows, nx),
        vmem(levels_x, *plane), vmem(levels_x, *plane), vmem(*plane),
        vmem(nx, rows), vmem(nx, rows),
        vmem(levels_y, ny, *tile), vmem(levels_y, ny, *tile), vmem(ny, *tile),
        vmem(ny, *tile), vmem(ny, *tile),
        vmem(levels_z, nz, ny, nx), vmem(levels_z, nz, ny, nx), vmem(nz, ny, nx),
        vmem(*plane), vmem(4 * ny, nx), vmem(4 * ny, nx),
        vmem(2, rows), vmem(1, rows), vmem(1, rows), vmem(2, rows),
        vmem(2, *tile), vmem(*tile), vmem(*tile), vmem(2, *tile),
        vmem(count_x, 4, rows), vmem(count_x, 2, rows),
        vmem(members, 4, *tile), vmem(groups, 4, *tile), vmem(count_y, *tile), vmem(4, *tile),
        vmem(members + groups, *tile), vmem(members + groups, *tile), vmem(12, *tile),
        dma(7), dma(2), dma(4), dma(4), pltpu.SemaphoreType.REGULAR((2,)),
    ]
    scratch += [pltpu.SemaphoreType.DMA] * 10
    anywhere = pl.BlockSpec(memory_space=pl.ANY)
    outs = pl.pallas_call(
        partial(kernel, sizes),
        out_shape=(
            jax.ShapeDtypeStruct(plane, f32),
            jax.ShapeDtypeStruct(plane, f32),
            jax.ShapeDtypeStruct((4 * rows, nx), f32),
        ),
        in_specs=[anywhere] * 6,
        out_specs=(pl.BlockSpec(memory_space=pltpu.VMEM), anywhere, anywhere),
        scratch_shapes=scratch,
        compiler_params=pltpu.CompilerParams(
            collective_id=0, has_side_effects=True, vmem_limit_bytes=24 << 20
        ),
        name="adi_step",
    )(
        *(
            pltpu.with_memory_space_constraint(a, pltpu.HBM)
            for a in (
                pressure.reshape(plane),
                fluid_flux.reshape(plane),
                memory.reshape(4 * rows, nx),
                lateral_faces.reshape(2 * rows, nx),
                vertical_faces.reshape(plane),
                relax_rates.reshape(4 * ny, nx),
            )
        )
    )
    step, flux, memory = outs
    next_pressure, next_flux, next_memory = pl.pallas_call(
        partial(last_relaxation, (nz, ny, nx)),
        out_shape=(
            jax.ShapeDtypeStruct(plane, f32),
            jax.ShapeDtypeStruct(plane, f32),
            jax.ShapeDtypeStruct((4 * rows, nx), f32),
        ),
        in_specs=[pl.BlockSpec(memory_space=pltpu.VMEM)] * 5,
        out_specs=(anywhere,) * 3,
        scratch_shapes=[
            vmem(*plane), vmem(*plane), vmem(4 * rows, nx), dma(3),
        ],
        compiler_params=pltpu.CompilerParams(vmem_limit_bytes=24 << 20),
        name="last_relaxation",
    )(step, flux, memory, pressure.reshape(plane), relax_rates.reshape(4 * ny, nx))
    return (
        next_pressure.reshape(nz, ny, nx),
        next_flux.reshape(nz, ny, nx),
        next_memory.reshape(4, nz, ny, nx),
    )


def solution(mesh):
    in_specs = (
        P(None, "gy", "gx"),
        P(None, "gy", "gx"),
        P(None, None, "gy", "gx"),
        P(None, None, "gy", "gx"),
        P(None, "gy", "gx"),
        P(None, "gy", "gx"),
    )
    out_specs = (P(None, "gy", "gx"), P(None, "gy", "gx"), P(None, None, "gy", "gx"))
    return jax.shard_map(
        partial(local, mesh), mesh=mesh, in_specs=in_specs, out_specs=out_specs, check_vma=False
    )
```

```python
from functools import partial

import jax
import jax.numpy as jnp
from jax import lax
from jax.experimental import pallas as pl
from jax.experimental.pallas import tpu as pltpu
from jax.sharding import PartitionSpec as P

MESH = pl.DeviceIdType.MESH


def rolled_low(a, s):
    return pltpu.roll(a, s, axis=1)


def rolled_high(a, s):
    return pltpu.roll(a, a.shape[1] - s, axis=1)


def major_low(a, s):
    return jnp.concatenate([a[a.shape[0] - s :], a[: a.shape[0] - s]], axis=0)


def major_high(a, s):
    return jnp.concatenate([a[s:], a[:s]], axis=0)


def factor(half, position, n, low, high, k1_ref, k2_ref, inv_ref, ends):
    first, last = position == 0, position == n - 1
    zero = jnp.zeros_like(half)
    link = jnp.where(last, zero, half)
    main = 1.0 + half + jnp.where(first, zero, low(half, 1))
    columns = []
    if ends:
        one = jnp.ones_like(half)
        columns = [jnp.where(first, one, zero), jnp.where(last, one, zero)]
    s, level = 1, 0
    while s < n:
        inverse = 1.0 / main
        k2 = link * high(inverse, s)
        scaled = link * inverse
        k1 = low(scaled, s)
        k1_ref[level] = k1
        k2_ref[level] = k2
        columns = [v + k1 * low(v, s) + k2 * high(v, s) for v in columns]
        main = main - low(link * scaled, s) - link * k2
        link = k2 * high(link, s)
        s, level = 2 * s, level + 1
    inverse = 1.0 / main
    inv_ref[...] = inverse
    return [v * inverse for v in columns]


def reduce_lines(right, n, low, high, k1_ref, k2_ref, inv_ref):
    s, level = 1, 0
    while s < n:
        right = right + k1_ref[level] * low(right, s) + k2_ref[level] * high(right, s)
        s, level = 2 * s, level + 1
    return right * inv_ref[...]


def join(one, two):
    g1, c1, w1, h1 = one
    g2, c2, w2, h2 = two
    e1 = 1.0 - w1 * h1
    gh = g2 * h1
    d = 1.0 / (1.0 + gh * e1)
    up, down = c1 * h1 * d, c2 * h1 * d
    return g1 + up * gh * c1, up * c2, w2 - down * e1 * c2, h2


def join_all(blocks, combine):
    while len(blocks) > 1:
        blocks = [combine(blocks[k], blocks[k + 1]) for k in range(0, len(blocks), 2)]
    return blocks[0]


def below(blocks, state):
    top, bottom, h = state
    factors, states = [], []
    for counts, (gj, cj, wj, hj) in blocks:
        states.append((top, bottom, h))
        a = h * (bottom - top * h)
        new_bottom = bottom + gj * a
        new_top = wj * new_bottom - cj * cj * a
        t = cj / new_bottom
        factors.append((t * h * bottom, t * a))
        top = jnp.where(counts, new_top, top)
        bottom = jnp.where(counts, new_bottom, bottom)
        h = jnp.where(counts, hj, h)
    return (top, bottom, h), factors, states


def above(blocks, state):
    top, bottom = state
    factors, states = [], []
    for counts, (gj, cj, wj, hj) in blocks:
        states.append((top, bottom))
        ch = cj * hj
        new_bottom = bottom + top * (hj * (1.0 - wj * hj))
        new_top = gj * new_bottom + ch * ch * top
        t = ch / new_bottom
        factors.append((t * bottom, t * top * hj))
        top = jnp.where(counts, new_top, top)
        bottom = jnp.where(counts, new_bottom, bottom)
    return (top, bottom), factors, states


def below_fractions(blocks, state):
    top, bottom, h = state
    factors = []
    for counts, (gj, cj, wj, hj) in blocks:
        a = h * (bottom - top * h)
        new_bottom = bottom + gj * a
        mixed = cj * a
        factors.append((new_bottom, cj * h, mixed))
        new_top = wj * new_bottom - cj * mixed
        top = jnp.where(counts, new_top, top)
        bottom = jnp.where(counts, new_bottom, bottom)
        h = jnp.where(counts, hj, h)
    return (top, bottom, h), factors


def above_fractions(blocks, state):
    top, bottom = state
    factors = []
    for counts, (gj, cj, wj, hj) in blocks:
        ch = cj * hj
        new_bottom = bottom + top * (hj * (1.0 - wj * hj))
        factors.append((new_bottom, ch, ch * hj * top))
        new_top = gj * new_bottom + ch * ch * top
        top = jnp.where(counts, new_top, top)
        bottom = jnp.where(counts, new_bottom, bottom)
    return (top, bottom), factors


def own_factors(own, low_state, high_state):
    g, c, w, h = own
    top, bottom, h_low = low_state
    a = h_low * (bottom - top * h_low) / bottom
    gh = high_state[0] * h / high_state[1]
    p = h / (1.0 + gh)
    q = gh * p
    r1, r2, ca, cq = 1.0 + g * a, 1.0 - w * q, c * a, c * q
    inverse = 1.0 / (r1 * r2 + ca * cq)
    return (h_low, a, p, q, r1 * inverse, r2 * inverse, ca * inverse, cq * inverse)


def inflow(own, factors, mine, e_low, f_high):
    g, c, w, _ = own
    h_low, a, p, q, r1, r2, ca, cq = factors
    u, v = h_low * e_low, p * f_high
    s1 = mine[0] + g * u + c * v
    s2 = mine[1] + c * u + w * v
    return u - a * (r2 * s1 + cq * s2), v + q * (r1 * s2 - ca * s1)


class Steps:
    def __init__(self, sizes, index):
        self.sizes, self.index = sizes, index
        self.count = 1
        for size in sizes:
            self.count *= size

    def split(self, number):
        digits = []
        for size in self.sizes[::-1]:
            digits.append(number % size)
            number = number // size
        return digits[::-1]

    def to(self, k):
        place = 0
        for size, at, step in zip(self.sizes, self.split(self.index), self.split(k)):
            place = place * size + (lax.rem(at + step, size) if step else at)
        return place

    def hops(self, k):
        return sum(min(step, size - step) for size, step in zip(self.sizes, self.split(k)))

    def far_first(self, least=1, most=99):
        steps = [k for k in range(1, self.count) if least <= self.hops(k) <= most]
        return sorted(steps, key=lambda k: -self.hops(k))


class Ring:
    def __init__(self, buffer, sems, steps, device, source=None):
        self.buffer, self.steps, self.device = buffer, steps, device
        self.send, self.receive = sems
        self.source = source or (lambda to: buffer.at[steps.index])

    def start(self, least=1, most=99):
        for k in self.steps.far_first(least, most):
            to = self.steps.to(k)
            pltpu.make_async_remote_copy(
                src_ref=self.source(to),
                dst_ref=self.buffer.at[self.steps.index],
                send_sem=self.send,
                recv_sem=self.receive,
                device_id=self.device(to),
                device_id_type=MESH,
            ).start()

    def all(self):
        every = self.buffer.at[pl.ds(0, self.steps.count - 1)]
        return pltpu.make_async_remote_copy(
            src_ref=every,
            dst_ref=every,
            send_sem=self.send,
            recv_sem=self.receive,
            device_id=self.device(self.steps.to(1)),
            device_id_type=MESH,
        )

    def arrive(self):
        self.all().wait_recv()

    def finish(self):
        self.all().wait_send()


def kernel(
    sizes,
    pressure_in, flux_in, memory_in, lateral_in, vertical_in, relax_in,
    step_out, flux_out, memory_out,
    p_ref, f_ref, m_ref, kx_ref, ky_ref, kz_ref, relax_ref,
    nf_ref, nm_ref,
    x1_ref, x2_ref, xi_ref, vt_ref, wt_ref,
    y1_ref, y2_ref, yi_ref, vs_ref, ws_ref,
    z1_ref, z2_ref, zi_ref,
    e_ref, iw_ref, wi_ref,
    east_out, west_out, east_in, west_in,
    north_out, south_out, north_in, south_in,
    xc_ref, xv_ref, yc_ref, yc2_ref, yv_ref, ys_ref,
    ylow_ref, yhigh_ref, yown_ref,
    load_sem, store_sem, halo_send, halo_receive, relay_sem,
    xc_send, xc_receive, xv_send, xv_receive,
    yc_send, yc_receive, yc2_send, yc2_receive, yv_send, yv_receive,
):
    nz, ny, nx, count_x, members, groups = sizes
    rows = nz * ny
    count_y = members * groups
    iy, ix = lax.axis_index("gy"), lax.axis_index("gx")
    group, member = iy // members, lax.rem(iy, members)
    reach = max(1, count_x // 4)
    beyond = count_x // 2 > reach
    along_x = Steps((count_x,), ix)
    along_y = Steps((4, 4, 2) if count_y == 32 else (count_y,), iy)
    inside = Steps((members // 2, 2), member)
    between = Steps((groups,), group)

    def at_x(k):
        return (iy, k)

    def at_y(k):
        return (k, ix)

    def in_group(k):
        return (group * members + k, ix)

    def across(k):
        return (k * members + member, ix)

    loads = [
        pltpu.make_async_copy(source, target, load_sem.at[k])
        for k, (source, target) in enumerate(
            [
                (pressure_in, p_ref),
                (lateral_in.at[pl.ds(0, rows)], kx_ref),
                (lateral_in.at[pl.ds(rows, rows)], ky_ref),
                (vertical_in, kz_ref),
                (flux_in, f_ref),
                (memory_in, m_ref),
                (relax_in, relax_ref),
            ]
        )
    ]
    for load in loads:
        load.start()

    barrier = pltpu.get_barrier_semaphore()

    north, south = lax.rem(iy + 1, count_y), lax.rem(iy + count_y - 1, count_y)
    east, west = lax.rem(ix + 1, count_x), lax.rem(ix + count_x - 1, count_x)
    greeted = [
        device(steps.to(k))
        for steps, device, most in (
            (along_x, at_x, reach), (between, across, 99), (inside, in_group, 99)
        )
        for k in steps.far_first(1, most)
    ] + [at_y(north), at_y(south)]
    for device in greeted:
        pl.semaphore_signal(barrier, inc=1, device_id=device, device_id_type=MESH)

    lanes = lax.broadcasted_iota(jnp.int32, (rows, nx), 1)
    zero_plane = jnp.zeros((rows, nx), jnp.float32)
    planes = (nz, ny, nx)

    def strided(ref, y):
        return ref[pl.ds(y, nz, stride=ny), :]

    for k in range(3):
        loads[k].wait()
    p = p_ref[...]
    kx = kx_ref[...]
    turned = jnp.transpose(jnp.where(lanes == 1, rolled_low(kx, 2), p))
    p_first, kx_last, p_last = turned[0:1], turned[1:2], turned[nx - 1 : nx]
    east_out[0:1] = p_last
    east_out[1:2] = kx_last
    west_out[...] = p_first
    north_out[0] = strided(p_ref, ny - 1)
    north_out[1] = strided(ky_ref, ny - 1)
    south_out[...] = strided(p_ref, 0)

    v, w = factor(0.5 * kx, lanes, nx, rolled_low, rolled_high, x1_ref, x2_ref, xi_ref, True)
    vt, wt = jnp.transpose(v), jnp.transpose(w)
    vt_ref[...] = vt
    wt_ref[...] = wt
    xc_ref[ix, 0:1] = vt[0:1]
    xc_ref[ix, 1:2] = vt[nx - 1 : nx]
    xc_ref[ix, 2:3] = wt[nx - 1 : nx]
    xc_ref[ix, 3:4] = 0.5 * kx_last

    half_y = 0.5 * jnp.stack([strided(ky_ref, y) for y in range(ny)])
    row = lax.broadcasted_iota(jnp.int32, half_y.shape, 0)
    vs, ws = factor(half_y, row, ny, major_low, major_high, y1_ref, y2_ref, yi_ref, True)
    vs_ref[...] = vs
    ws_ref[...] = ws
    yc_ref[member, 0] = vs[0]
    yc_ref[member, 1] = vs[ny - 1]
    yc_ref[member, 2] = ws[ny - 1]
    yc_ref[member, 3] = half_y[ny - 1]

    for k in range(3, 7):
        loads[k].wait()
    kz = kz_ref[...]
    half_z = 0.5 * kz.reshape(planes)
    plane = lax.broadcasted_iota(jnp.int32, planes, 0)
    factor(half_z, plane, nz, major_low, major_high, z1_ref, z2_ref, zi_ref, False)
    p = p_ref[...]
    kx = kx_ref[...]
    explicit = kx * (jnp.where(lanes == nx - 1, zero_plane, rolled_high(p, 1)) - p)
    explicit -= jnp.where(
        lanes == 0, zero_plane, rolled_low(kx, 1) * (p - rolled_low(p, 1))
    )
    gap = jnp.zeros((ny, nx), jnp.float32)
    flow = kz * (jnp.concatenate([p[ny:], gap], axis=0) - p)
    explicit += flow - jnp.concatenate([gap, flow[: rows - ny]], axis=0)
    memory = m_ref[...].reshape(4, rows, nx)
    e_ref[...] = explicit + (f_ref[...] - (memory[0] + memory[1] + memory[2] + memory[3]))
    previous = None
    for y in range(ny):
        k_here, p_here = strided(ky_ref, y), strided(p_ref, y)
        p_next = strided(p_ref, y + 1) if y + 1 < ny else jnp.zeros_like(p_here)
        flow = k_here * (p_next - p_here)
        along = flow if previous is None else flow - previous
        e_ref[pl.ds(y, nz, stride=ny), :] = strided(e_ref, y) + along
        previous = flow
    weight = relax_ref[...]
    inverse = 1.0 / (1.0 + weight)
    iw_ref[...] = inverse
    wi_ref[...] = weight * inverse

    def halo(k, source, target, device):
        return pltpu.make_async_remote_copy(
            src_ref=source,
            dst_ref=target,
            send_sem=halo_send.at[k],
            recv_sem=halo_receive.at[k],
            device_id=device,
            device_id_type=MESH,
        )

    halos = [
        halo(0, east_out, west_in, (iy, east)),
        halo(1, west_out, east_in, (iy, west)),
        halo(2, north_out, south_in, (north, ix)),
        halo(3, south_out, north_in, (south, ix)),
    ]
    xc = Ring(xc_ref, (xc_send, xc_receive), along_x, at_x)
    xv = Ring(xv_ref, (xv_send, xv_receive), along_x, at_x)
    yc = Ring(yc_ref, (yc_send, yc_receive), inside, in_group)
    yc2 = Ring(yc2_ref, (yc2_send, yc2_receive), between, across)

    pl.semaphore_wait(barrier, len(greeted))
    if beyond:
        for far in (lax.rem(ix + reach, count_x), lax.rem(ix + count_x - reach, count_x)):
            pl.semaphore_signal(
                relay_sem.at[0], inc=1, device_id=(iy, far), device_id_type=MESH
            )
    for copy in halos:
        copy.start()
    for k in between.far_first():
        pl.semaphore_signal(
            relay_sem.at[1], inc=1, device_id=across(between.to(k)), device_id_type=MESH
        )
    xc.start(1, reach)
    yc.start()

    halos[2].wait_recv()
    halos[3].wait_recv()
    p_south = strided(p_ref, 0)
    k_north = strided(ky_ref, ny - 1)
    from_south = south_in[1] * (south_in[0] - p_south)
    from_south = jnp.where(iy == 0, jnp.zeros_like(from_south), from_south)
    from_north = k_north * north_in[...]
    from_north = jnp.where(iy == count_y - 1, jnp.zeros_like(from_north), from_north)
    e_ref[pl.ds(0, nz, stride=ny), :] = strided(e_ref, 0) + from_south
    e_ref[pl.ds(ny - 1, nz, stride=ny), :] = strided(e_ref, ny - 1) + from_north
    halos[0].wait_recv()
    halos[1].wait_recv()
    from_west = west_in[1:2] * (west_in[0:1] - west_out[...])
    from_west = jnp.where(ix == 0, jnp.zeros_like(from_west), from_west)
    from_east = east_out[1:2] * east_in[...]
    from_east = jnp.where(ix == count_x - 1, jnp.zeros_like(from_east), from_east)
    line = lax.broadcasted_iota(jnp.int32, (nx, rows), 0)
    edges = jnp.where(line == 0, from_west, jnp.where(line == nx - 1, from_east, 0.0))
    explicit = e_ref[...] + jnp.transpose(edges)

    step_z = reduce_lines(
        explicit.reshape(planes), nz, major_low, major_high, z1_ref, z2_ref, zi_ref
    )

    right = step_z.reshape(rows, nx)
    turned = jnp.transpose(right)
    xv_ref[ix, 0:1] = jnp.sum(vt_ref[...] * turned, axis=0, keepdims=True)
    xv_ref[ix, 1:2] = jnp.sum(wt_ref[...] * turned, axis=0, keepdims=True)
    if beyond:
        pl.semaphore_wait(relay_sem.at[0], 2)
        for hops in range(count_x // 2, reach, -1):
            xc.start(hops, hops)
            xv.start(hops, hops)
    xv.start(1, reach)

    yc.arrive()

    def y_block(j):
        return tuple(yc_ref[j, k] for k in range(4))

    whole = join_all([y_block(j) for j in range(members)], join)
    for k in range(4):
        yc2_ref[group, k] = whole[k]
    yc2.start()

    def saturated(d):
        return d * lax.rsqrt(1.0 + d * d)

    def relaxed(memory, d):
        target = saturated(d).reshape(1, nz, ny, nx)
        share = wi_ref[...].reshape(4, 1, ny, nx)
        return memory * iw_ref[...].reshape(4, 1, ny, nx) + share * target

    local_x = reduce_lines(right, nx, rolled_low, rolled_high, x1_ref, x2_ref, xi_ref)
    nm_ref[...] = relaxed(m_ref[...].reshape(4, nz, ny, nx), step_z).reshape(4 * rows, nx)
    e_ref[...] = local_x

    yc2.arrive()

    def y_group(j):
        return tuple(yc2_ref[j, k] for k in range(4))

    own_y = tuple(yc_ref[member, k] for k in range(4))
    zero, one = jnp.zeros_like(own_y[0]), jnp.ones_like(own_y[0])
    state, lows, _ = below([(j < group, y_group(j)) for j in range(groups - 1)], (zero, one, zero))
    _, low_members, low_states = below([(True, y_block(j)) for j in range(members)], state)
    uppers = list(range(groups - 1, 0, -1))
    state, highs, _ = above([(j > group, y_group(j)) for j in uppers], (zero, one))
    downward = list(range(members - 1, -1, -1))
    _, high_members, high_states = above([(True, y_block(j)) for j in downward], state)
    high_members, high_states = high_members[::-1], high_states[::-1]
    low_state, high_state = low_states[0], high_states[0]
    low_own, high_own = low_members[0], high_members[0]
    for j in range(1, members):
        low_state, high_state, low_own, high_own = jax.tree.map(
            lambda new, old: jnp.where(member == j, new, old),
            (low_states[j], high_states[j], low_members[j], high_members[j]),
            (low_state, high_state, low_own, high_own),
        )
    past_above, past_below = one, one
    for j in range(members):
        past_above = jnp.where(j > member, past_above * low_members[j][0], past_above)
        past_below = jnp.where(j < member, past_below * high_members[j][0], past_below)
    for n in range(members):
        ylow_ref[groups + n] = low_members[n][0]
        yhigh_ref[groups + n] = high_members[n][0]
    for n in range(groups - 1):
        ylow_ref[n] = lows[n][0]
        yhigh_ref[n] = highs[n][0]
    own_parts = own_factors(own_y, low_state, high_state)
    own_parts += (low_own[1], high_own[1], past_above, past_below)
    for n, part in enumerate(own_parts):
        yown_ref[n] = part

    xc.arrive()

    def x_block(j):
        return tuple(xc_ref[j, k : k + 1] for k in range(4))

    own_x = tuple(xc_ref[ix, k : k + 1] for k in range(4))
    zero, one = jnp.zeros_like(own_x[0]), jnp.ones_like(own_x[0])
    x_lower = [(j < ix, j) for j in range(count_x - 1)]
    x_upper = [(j > ix, j) for j in range(count_x - 1, 0, -1)]
    low_state, lows = below_fractions([(c, x_block(j)) for c, j in x_lower], (zero, one, zero))
    high_state, highs = above_fractions([(c, x_block(j)) for c, j in x_upper], (zero, one))
    factors = own_factors(own_x, low_state, high_state)
    low_bottom, high_bottom = 1.0 / low_state[1], 1.0 / high_state[1]

    xv.arrive()
    e_low, f_high = zero, zero
    for (counts, j), (bottom, past, mixed) in zip(x_lower, lows):
        got = bottom * xv_ref[j, 1:2] - mixed * xv_ref[j, 0:1] + past * e_low
        e_low = jnp.where(counts, got, e_low)
    for (counts, j), (bottom, past, mixed) in zip(x_upper, highs):
        got = bottom * xv_ref[j, 0:1] + mixed * xv_ref[j, 1:2] + past * f_high
        f_high = jnp.where(counts, got, f_high)
    e_low, f_high = e_low * low_bottom, f_high * high_bottom
    mine = (xv_ref[ix, 0:1], xv_ref[ix, 1:2])
    lower_in, upper_in = inflow(own_x, factors, mine, e_low, f_high)
    step_x = e_ref[...] + jnp.transpose(vt_ref[...] * lower_in + wt_ref[...] * upper_in)

    e_ref[...] = step_x
    right = jnp.stack([strided(e_ref, y) for y in range(ny)])
    first = jnp.sum(vs_ref[...] * right, axis=0)
    last = jnp.sum(ws_ref[...] * right, axis=0)
    upward = last - yown_ref[8] * first
    downwards = first + yown_ref[9] * last
    ys_ref[0], ys_ref[1] = downwards, upward
    ys_ref[2], ys_ref[3] = downwards * yown_ref[11], upward * yown_ref[10]
    yv_ref[iy] = jnp.zeros_like(first)

    def toward(to):
        outside = jnp.where(to // members == group, 0, 2)
        return ys_ref.at[outside + jnp.where(to > iy, 1, 0)]

    yv = Ring(yv_ref, (yv_send, yv_receive), along_y, at_y, toward)
    if groups > 1:
        pl.semaphore_wait(relay_sem.at[1], groups - 1)
    yv.start()

    yi_ref[...] = reduce_lines(right, ny, major_low, major_high, y1_ref, y2_ref, yi_ref)
    memory = m_ref[...].reshape(4, rows, nx)
    partly = relaxed(nm_ref[...].reshape(4, nz, ny, nx), e_ref[...])
    partly = (partly * iw_ref[...].reshape(4, 1, ny, nx)).reshape(4, rows, nx)
    nm_ref[...] = partly.reshape(4 * rows, nx)
    moved = partly - memory
    nf_ref[...] = f_ref[...] - (moved[0] + moved[1] + moved[2] + moved[3])
    stores = [
        pltpu.make_async_copy(nm_ref, memory_out, store_sem.at[0]),
        pltpu.make_async_copy(nf_ref, flux_out, store_sem.at[1]),
    ]
    for store in stores:
        store.start()

    yv.arrive()
    e_low, f_high = jnp.zeros_like(first), jnp.zeros_like(first)
    sums = []
    for j in range(groups):
        parts = [yv_ref[j * members + k] for k in range(members)]
        sums.append(join_all(parts, lambda a, b: a + b))
    for j in range(groups - 1):
        e_low = jnp.where(j < group, sums[j] + ylow_ref[j] * e_low, e_low)
    for n, j in enumerate(uppers):
        f_high = jnp.where(j > group, sums[j] + yhigh_ref[n] * f_high, f_high)
    for j in range(members - 1):
        got = yv_ref[group * members + j] + ylow_ref[groups + j] * e_low
        e_low = jnp.where(j < member, got, e_low)
    for j in downward[:-1]:
        got = yv_ref[group * members + j] + yhigh_ref[groups + j] * f_high
        f_high = jnp.where(j > member, got, f_high)
    own_y = tuple(yc_ref[member, k] for k in range(4))
    factors = tuple(yown_ref[n] for n in range(8))
    lower_in, upper_in = inflow(own_y, factors, (first, last), e_low, f_high)
    step_y = yi_ref[...] + vs_ref[...] * lower_in + ws_ref[...] * upper_in
    for y in range(ny):
        step_out[pl.ds(y, nz, stride=ny), :] = step_y[y]
    for copy in halos:
        copy.wait_send()
    for ring in (xc, yc, xv, yc2, yv):
        ring.finish()
    for store in stores:
        store.wait()


def last_relaxation(
    sizes, step_ref, flux_ref, memory_ref, pressure_ref, relax_ref,
    pressure_out, flux_out, memory_out,
    p_ref, f_ref, m_ref, store_sem,
):
    nz, ny, nx = sizes
    rows = nz * ny
    pairs = [(p_ref, pressure_out), (m_ref, memory_out), (f_ref, flux_out)]
    stores = [pltpu.make_async_copy(a, b, store_sem.at[k]) for k, (a, b) in enumerate(pairs)]
    step = step_ref[...]
    target = (step * lax.rsqrt(1.0 + step * step)).reshape(nz, ny, nx)
    weight = relax_ref[...].reshape(4, 1, ny, nx)
    share = weight / (1.0 + weight)
    memory = memory_ref[...].reshape(4, nz, ny, nx) + share * target[None]
    m_ref[...] = memory.reshape(4 * rows, nx)
    stores[1].start()
    p_ref[...] = pressure_ref[...] + step
    stores[0].start()
    shares = (share[0] + share[1]) + (share[2] + share[3])
    f_ref[...] = flux_ref[...] - (shares * target).reshape(rows, nx)
    stores[2].start()
    for store in stores:
        store.wait()


def local(mesh, pressure, fluid_flux, memory, lateral_faces, vertical_faces, relax_rates):
    nz, ny, nx = pressure.shape
    rows = nz * ny
    count_y, count_x = mesh.shape["gy"], mesh.shape["gx"]
    groups = 4 if count_y >= 16 else max(1, count_y // 2)
    members = count_y // groups
    sizes = (nz, ny, nx, count_x, members, groups)
    f32 = jnp.float32

    def vmem(*shape):
        return pltpu.VMEM(shape, f32)

    def dma(n):
        return pltpu.SemaphoreType.DMA((max(n, 1),))

    plane = (rows, nx)
    levels_x, levels_y, levels_z = (n.bit_length() - 1 for n in (nx, ny, nz))
    tile = (nz, nx)
    scratch = [
        vmem(*plane), vmem(*plane), vmem(4 * rows, nx), vmem(*plane), vmem(*plane),
        vmem(*plane), vmem(4 * ny, nx),
        vmem(*plane), vmem(4 * rows, nx),
        vmem(levels_x, *plane), vmem(levels_x, *plane), vmem(*plane),
        vmem(nx, rows), vmem(nx, rows),
        vmem(levels_y, ny, *tile), vmem(levels_y, ny, *tile), vmem(ny, *tile),
        vmem(ny, *tile), vmem(ny, *tile),
        vmem(levels_z, nz, ny, nx), vmem(levels_z, nz, ny, nx), vmem(nz, ny, nx),
        vmem(*plane), vmem(4 * ny, nx), vmem(4 * ny, nx),
        vmem(2, rows), vmem(1, rows), vmem(1, rows), vmem(2, rows),
        vmem(2, *tile), vmem(*tile), vmem(*tile), vmem(2, *tile),
        vmem(count_x, 4, rows), vmem(count_x, 2, rows),
        vmem(members, 4, *tile), vmem(groups, 4, *tile), vmem(count_y, *tile), vmem(4, *tile),
        vmem(members + groups, *tile), vmem(members + groups, *tile), vmem(12, *tile),
        dma(7), dma(2), dma(4), dma(4), pltpu.SemaphoreType.REGULAR((2,)),
    ]
    scratch += [pltpu.SemaphoreType.DMA] * 10
    anywhere = pl.BlockSpec(memory_space=pl.ANY)
    outs = pl.pallas_call(
        partial(kernel, sizes),
        out_shape=(
            jax.ShapeDtypeStruct(plane, f32),
            jax.ShapeDtypeStruct(plane, f32),
            jax.ShapeDtypeStruct((4 * rows, nx), f32),
        ),
        in_specs=[anywhere] * 6,
        out_specs=(pl.BlockSpec(memory_space=pltpu.VMEM), anywhere, anywhere),
        scratch_shapes=scratch,
        compiler_params=pltpu.CompilerParams(
            collective_id=0, has_side_effects=True, vmem_limit_bytes=24 << 20
        ),
        name="adi_step",
    )(
        *(
            pltpu.with_memory_space_constraint(a, pltpu.HBM)
            for a in (
                pressure.reshape(plane),
                fluid_flux.reshape(plane),
                memory.reshape(4 * rows, nx),
                lateral_faces.reshape(2 * rows, nx),
                vertical_faces.reshape(plane),
                relax_rates.reshape(4 * ny, nx),
            )
        )
    )
    step, flux, memory = outs
    next_pressure, next_flux, next_memory = pl.pallas_call(
        partial(last_relaxation, (nz, ny, nx)),
        out_shape=(
            jax.ShapeDtypeStruct(plane, f32),
            jax.ShapeDtypeStruct(plane, f32),
            jax.ShapeDtypeStruct((4 * rows, nx), f32),
        ),
        in_specs=[pl.BlockSpec(memory_space=pltpu.VMEM)] * 5,
        out_specs=(anywhere,) * 3,
        scratch_shapes=[
            vmem(*plane), vmem(*plane), vmem(4 * rows, nx), dma(3),
        ],
        compiler_params=pltpu.CompilerParams(vmem_limit_bytes=24 << 20),
        name="last_relaxation",
    )(step, flux, memory, pressure.reshape(plane), relax_rates.reshape(4 * ny, nx))
    return (
        next_pressure.reshape(nz, ny, nx),
        next_flux.reshape(nz, ny, nx),
        next_memory.reshape(4, nz, ny, nx),
    )


def solution(mesh):
    in_specs = (
        P(None, "gy", "gx"),
        P(None, "gy", "gx"),
        P(None, None, "gy", "gx"),
        P(None, None, "gy", "gx"),
        P(None, "gy", "gx"),
        P(None, "gy", "gx"),
    )
    out_specs = (P(None, "gy", "gx"), P(None, "gy", "gx"), P(None, None, "gy", "gx"))
    return jax.shard_map(
        partial(local, mesh), mesh=mesh, in_specs=in_specs, out_specs=out_specs, check_vma=False
    )
```
